32 devices in a mesh: dev: 32 (over z, y, x, core).
Axes of the slice: x: 2, y: 2, z: 4, core: 2. Of those that a mesh axis runs over, the one named last changes fastest.
Arguments:
- positions: float32 [3, 131072], P(None, 'dev'), may hold values from 0 to 1
- velocities: float32 [3, 131072], P(None, 'dev'), may hold values from -3 to 3
- masses: float32 [131072], P('dev'), may hold values from 0.25 to 4
- samples: float32 [3, 1048576], P(None, 'dev'), may hold values from 0 to 1
- sample_mass: float32 [1048576], P('dev'), may hold values from 0.5 to 2
- start_potential: float32 [1048576], P('dev'), may hold values from -0.1 to 2.9
- route_owner: int32 [1024, 4], P('dev'), may hold values from 0 to 31, all different within a row; in each aligned block of 32 rows (0 to 31, 32 to 63, ...) at most 8 rows name the same one
- route_tile: int32 [1024, 4], P('dev'), may hold values from 0 to 63
- live_count: int32 [1024], P('dev'), may hold values from 3 to 4
Outputs:
- new_position: float32 [3, 131072], P(None, 'dev')
- new_velocity: float32 [3, 131072], P(None, 'dev')
The draws below stay inside these ranges and needn't reach their ends.
Inputs may be any that keep to these rules, and one draw needn't show every extreme that they name: `route_owner`: each row names 4 different devices; among the 32 rows of one device no device is named more than 8 times, and some device is named exactly 8 times.
All inputs are finite; a program needn't handle non-finite values.
Results may differ from the reference program's by a relative error of at most 0.0003.
Values sent between devices are 32-bit elements; how exact they have to be, the bound alone decides.
No kernel may reach another device: no remote copies, remote signals or barrier semaphores. Data moves between devices by JAX's collectives and lax.ppermute only.
A program may use at most 64 MiB of HBM per device.

```python
import math
import jax
import jax.numpy as jnp
import numpy as np
from jax import lax

BLK = 128
TILE = 512
K = 4
ITERS = 2
PB_DEV = 32
NT_DEV = 64
BLOCKS = 1024
TILES = 2048
PARTICLES = 131072
SAMPLES = 1048576
CAP = 8
N_DEV = 32


def draw_samples(key, part):
    base = jax.random.uniform(jax.random.fold_in(key, 23), (3, TILES, TILE), jnp.float32, 0.0, 1.0)
    return base.reshape(3, SAMPLES)


def draw_start_potential(key, part):
    noise_key = jax.random.fold_in(jax.random.fold_in(key, 17), 0)
    base = 0.02 * jax.random.truncated_normal(noise_key, -4.0, 4.0, (TILES, TILE), jnp.float32)
    return base.reshape(SAMPLES)


def with_ends(result, own_key, smallest, high):
    index_at = [jax.random.randint(jax.random.fold_in(own_key, axis), (), 0, length) for axis, length in enumerate(result.shape)]
    widest = result.shape.index(max(result.shape))
    next_to = index_at[:widest] + [(index_at[widest] + 1) % result.shape[widest]] + index_at[widest + 1:]
    return result.at[tuple(index_at)].set(smallest).at[tuple(next_to)].set(high)


def block_scale(rng, extent, shards, least, largest):
    level = 1.0
    for position, shards_of in shards:
        draws = jax.random.uniform(jax.random.fold_in(jax.random.fold_in(rng, 6), position), (shards_of,), jnp.float32, least / len(shards), largest / len(shards))
        level = level * jnp.repeat(jnp.exp(draws), extent[position] // shards_of).reshape((-1,) + (1,) * (len(extent) - 1 - position))
    return level


def shared_out(own_key, own, number, rows, amount, top, most, lean):
    sequence = jax.random.permutation(own_key, amount)
    heavy_load, common = portions_of(amount, rows * top, most, lean, True), portions_of(amount, rows * top, most, lean, False)
    places = jnp.arange(amount)

    def named(tallies, rotation):
        used = int((tallies > 0).sum())
        fixed = max(1, used // 4)
        passed = fixed + (places - fixed + rotation * (used - fixed)) % max(1, amount - fixed)
        return jnp.zeros((amount,), jnp.int32).at[sequence[jnp.where(places < fixed, places, passed)]].set(jnp.asarray(tallies, jnp.int32))

    tallies = jnp.where(number % 4 == 0, named(heavy_load, number // 4), named(common, number - number // 4 - 1))
    mixed = jax.random.permutation(jax.random.fold_in(own, 3), amount)
    donor, sink = mixed[0:amount // 2 * 2:2], mixed[1:amount // 2 * 2:2]
    margin = jnp.minimum(tallies[donor] - 1, most - tallies[sink]) // 2
    margin = jnp.where((donor == sequence[0]) | (sink == sequence[0]) | (tallies[sink] == 0), 0, jnp.maximum(margin, 0))
    passed = jax.random.randint(jax.random.fold_in(own, 4), (amount // 2,), 0, 1 << 20) % (margin + 1)
    tallies = tallies.at[donor].add(-passed).at[sink].add(passed)
    labels = jnp.searchsorted(jnp.cumsum(tallies), jnp.arange(rows * top), side="right").astype(jnp.int32)
    table = labels.reshape(top, rows).T
    table = table[jax.random.permutation(jax.random.fold_in(own, 1), rows)]
    rotation = jax.random.randint(jax.random.fold_in(own, 2), (rows, 1), 0, top)
    return jnp.take_along_axis(table, (jnp.arange(top)[None, :] + rotation) % top, axis=1)


def portions_of(count, total, bound, lean, full):
    loads = [(1 << 20) // math.isqrt(rank ** lean) + 1 for rank in range(1, count + 1)]
    largest = bound if full else min(bound, max(-(-total // count), total * loads[0] // sum(loads)))
    least = 1 if total - largest >= count - 1 else 0
    holding, surplus = [largest] + [least] * (count - 1), total - largest - least * (count - 1)
    while surplus > 0:
        movable = [i for i in range(1, count) if holding[i] < largest] or [i for i in range(1, count) if holding[i] < bound]
        mass, budget = sum([loads[i] for i in movable]), surplus
        for i in movable:
            addition = min(bound - holding[i], max(1, budget * loads[i] // mass), surplus)
            holding[i] = holding[i] + addition
            surplus = surplus - addition
    return np.array(holding)


def bell_draw(key, dims, scale, most, cuts=(), kind=jnp.bfloat16):
    values = jax.random.normal(key, dims, jnp.float32) * scale
    if len(cuts) > 0:
        values = block_scale(key, dims, cuts, -0.22, 0.18) * values
    return jnp.clip(values, min=-most, max=most).astype(kind)


def setup_inputs(seed: int = 0) -> dict:
    key_of = jax.random.split(jax.random.key(seed), 10)
    positions = jnp.clip(1.0 * jax.random.uniform(key_of[0], (3, PARTICLES), jnp.float32) ** block_scale(key_of[0], (3, PARTICLES), ((1, 32),), -0.2, 0.2), 0.0, 1.0)
    velocities = bell_draw(key_of[1], (3, PARTICLES), 0.5, 3.0, ((1, 32),), jnp.float32)
    masses = jnp.clip(jnp.exp(math.log(4.0) - 2.7725887 * jax.random.uniform(key_of[2], (PARTICLES,), jnp.float32) ** block_scale(key_of[2], (PARTICLES,), ((0, 32),), -0.2, 0.2)), 0.25, 4.0)
    samples = draw_samples(jax.random.fold_in(key_of[9], 71), 0)
    sample_mass = jnp.clip(jnp.exp(math.log(2.0) - 1.3862944 * jax.random.uniform(key_of[4], (SAMPLES,), jnp.float32) ** block_scale(key_of[4], (SAMPLES,), ((0, 32),), -0.2, 0.2)), 0.5, 2.0)
    start_potential = draw_start_potential(jax.random.fold_in(key_of[9], 71), 0)
    route_owner_keys = jax.random.split(jax.random.fold_in(key_of[6], 1), BLOCKS // PB_DEV)
    route_owner_turns = jax.random.permutation(jax.random.fold_in(key_of[6], 3), BLOCKS // PB_DEV)
    route_owner = jax.vmap(lambda own, number: shared_out(jax.random.fold_in(key_of[6], 2), own, number, PB_DEV, N_DEV, K, CAP, 2))(route_owner_keys, route_owner_turns).reshape((BLOCKS, K))
    route_tile = with_ends(jax.random.randint(key_of[7], (BLOCKS, K), 0, NT_DEV), jax.random.fold_in(key_of[7], 1), 0, NT_DEV - 1).astype(jnp.int32)
    live_count = with_ends(jax.random.randint(key_of[8], (BLOCKS,), 3, K + 1), jax.random.fold_in(key_of[8], 1), 3, K).astype(jnp.int32)
    return dict(positions=positions, velocities=velocities, masses=masses, samples=samples, sample_mass=sample_mass, start_potential=start_potential, route_owner=route_owner, route_tile=route_tile, live_count=live_count)


EPSILON = 0.01
STIFFNESS = 150.0
TIMESTEP = 0.05
NEGATIVE = -1.0e30
HIGHEST = lax.Precision.HIGHEST


def pair_costs(block_coordinates, tile_coordinates):
    first = block_coordinates[0][None, :, None] - tile_coordinates[:, 0][:, None, :]
    second = block_coordinates[1][None, :, None] - tile_coordinates[:, 1][:, None, :]
    third = block_coordinates[2][None, :, None] - tile_coordinates[:, 2][:, None, :]
    return 0.5 * (first * first + second * second + third * third)


def row_lse(score, active_mask):
    masked = jnp.where(active_mask[:, None, None], score, NEGATIVE)
    top = jnp.max(masked, axis=(0, 2))
    total = jnp.sum(jnp.exp(masked - top[None, :, None]), axis=(0, 2))
    return top + jnp.log(total)


def transport_block_update(block_coordinates, logarithm_masses, tile_coordinates, tile_dual_values, active_mask):
    cost = pair_costs(block_coordinates, tile_coordinates)
    row_dual_values = EPSILON * logarithm_masses - EPSILON * row_lse((tile_dual_values[:, None, :] - cost) / EPSILON, active_mask)
    score = (row_dual_values[None, :, None] - cost) / EPSILON
    column_peak = jnp.max(score, axis=1)
    column_total_sum = jnp.sum(jnp.exp(score - column_peak[:, None, :]), axis=1)
    return row_dual_values, jnp.where(active_mask[:, None], column_peak, NEGATIVE), jnp.where(active_mask[:, None], column_total_sum, 0.0)


def centre_block(block_coordinates, tile_coordinates, tile_dual_values, active_mask):
    cost = pair_costs(block_coordinates, tile_coordinates)
    masked = jnp.where(active_mask[:, None, None], (tile_dual_values[:, None, :] - cost) / EPSILON, NEGATIVE)
    top = jnp.max(masked, axis=(0, 2))
    weight = jnp.exp(masked - top[None, :, None])
    total = jnp.sum(weight, axis=(0, 2))
    numer = jnp.einsum("kij,kdj->di", weight, tile_coordinates, precision=HIGHEST)
    return numer / total[None, :]


def reference(positions, velocities, masses, samples, sample_mass, start_potential, route_owner, route_tile, live_count):
    block_coordinates = positions.reshape(3, BLOCKS, BLK).transpose(1, 0, 2)
    logarithm_masses = jnp.log(masses).reshape(BLOCKS, BLK)
    tile_coordinates = samples.reshape(3, TILES, TILE).transpose(1, 0, 2)
    log_sample = jnp.log(sample_mass).reshape(TILES, TILE)
    tile_ids = (route_owner * NT_DEV + route_tile).astype(jnp.int32)
    active_mask = jnp.arange(K, dtype=jnp.int32)[None, :] < live_count[:, None]
    dual_variable = start_potential.reshape(TILES, TILE)
    for step in range(ITERS):
        def visit(carry, item, dual_variable=dual_variable):
            top_acc, sum_acc = carry
            point_coordinates, logarithm_weight, particle_labels, surviving_flags = item
            row_dual_values, column_peak, column_total_sum = transport_block_update(point_coordinates, logarithm_weight, tile_coordinates[particle_labels], dual_variable[particle_labels], surviving_flags)
            for slot in range(K):
                target = particle_labels[slot]
                old_top = top_acc[target]
                new_top = jnp.maximum(old_top, column_peak[slot])
                new_sum = sum_acc[target] * jnp.exp(old_top - new_top) + column_total_sum[slot] * jnp.exp(column_peak[slot] - new_top)
                top_acc = top_acc.at[target].set(new_top)
                sum_acc = sum_acc.at[target].set(new_sum)
            return (top_acc, sum_acc), None

        start = (jnp.full((TILES, TILE), NEGATIVE, jnp.float32), jnp.zeros((TILES, TILE), jnp.float32))
        (top_acc, sum_acc), unused = lax.scan(visit, start, (block_coordinates, logarithm_masses, tile_ids, active_mask))
        covered = sum_acc > 0
        updated = EPSILON * log_sample - EPSILON * (top_acc + jnp.log(jnp.where(covered, sum_acc, 1.0)))
        dual_variable = jnp.where(covered, updated, dual_variable)

    def centre_of(item):
        return centre_block(item[0], tile_coordinates[item[1]], dual_variable[item[1]], item[2])

    centres = lax.map(centre_of, (block_coordinates, tile_ids, active_mask))
    centre = centres.transpose(1, 0, 2).reshape(3, BLOCKS * BLK)
    new_velocity = velocities + STIFFNESS * (centre - positions)
    new_position = positions + TIMESTEP * new_velocity
    return new_position, new_velocity
```

```python
import functools
import jax
import jax.numpy as jnp
from jax import lax
from jax.experimental import pallas as pl
from jax.experimental.pallas import tpu as pltpu
from jax.sharding import PartitionSpec as P

BLK = 128
TILE = 512
K = 4
CHUNKS = TILE // BLK
EPSILON = 0.01
STIFFNESS = 150.0
TIMESTEP = 0.05
LOG2E = 1.4426950408889634
SCALE = LOG2E / EPSILON
NEGATIVE = -1e30
ROW_SHIFT = 115.0
COL_SHIFT = 110.0
G = 8
ROWS = 4
DEPTH = 32

f32 = jnp.float32
bf16 = jnp.bfloat16
VMEM = pl.BlockSpec(memory_space=pltpu.VMEM)
SMEM = pl.BlockSpec(memory_space=pltpu.SMEM)


def call(kernel, out_shape, in_specs, out_specs, scratch, flops, args):
    size = sum(a.size * a.dtype.itemsize for a in args)
    return pl.pallas_call(
        kernel,
        out_shape=out_shape,
        in_specs=in_specs,
        out_specs=out_specs,
        scratch_shapes=scratch,
        compiler_params=pltpu.CompilerParams(vmem_limit_bytes=56 * 2**20),
        cost_estimate=pl.CostEstimate(flops=flops, bytes_accessed=size, transcendentals=0),
    )(*args)


def split3(value):
    high = value.astype(bf16).astype(f32)
    rest = value - high
    middle = rest.astype(bf16).astype(f32)
    return high, middle, rest - middle


def setup_kernel(capacity, owner_ref, tile_ref, live_ref, pos_ref, send_ref, slot_ref, count_ref):
    blocks = owner_ref.shape[0]

    def clear(i, carry):
        count_ref[i] = 0
        return carry

    lax.fori_loop(0, count_ref.shape[0], clear, 0)
    send_ref[...] = jnp.full(send_ref.shape, -1.0, f32)
    for b in range(blocks):
        rows = [pos_ref[d : d + 1, b * BLK : (b + 1) * BLK] for d in range(3)]
        for k in range(K):
            owner = owner_ref[b, k]
            rank = count_ref[owner]
            count_ref[owner] = rank + 1
            slot = owner * capacity + rank
            slot_ref[b * K + k] = slot
            tile = jnp.where(k < live_ref[b], tile_ref[b, k], -1).astype(f32)
            for d in range(3):
                send_ref[pl.ds(slot * ROWS + d, 1), :] = rows[d]
            send_ref[pl.ds(slot * ROWS + 3, 1), :] = jnp.full((1, BLK), tile, f32)


def home_gather(slot_ref, live_ref, recv_ref, parts_ref, filler):
    blocks = live_ref.shape[0]
    for b in range(blocks):
        live = live_ref[b]
        for k in range(K):
            row = recv_ref[pl.ds(slot_ref[b * K + k], 1), :]
            parts_ref[k, b : b + 1, :] = jnp.where(k < live, row, filler)


def home_scatter(slot_ref, rows_ref, send_ref):
    for b in range(rows_ref.shape[0]):
        row = rows_ref[b : b + 1, :]
        for k in range(K):
            send_ref[pl.ds(slot_ref[b * K + k], 1), :] = row


def home_first_kernel(slot_ref, live_ref, recv_ref, mass_ref, send_ref, row_ref, parts_ref):
    home_gather(slot_ref, live_ref, recv_ref, parts_ref, NEGATIVE)
    parts = parts_ref[...]
    top = jnp.max(parts, axis=0)
    total = jnp.sum(jnp.exp2(parts - top[None]), axis=0)
    row_ref[...] = jnp.log2(mass_ref[...]) - (top + jnp.log2(total))
    home_scatter(slot_ref, row_ref, send_ref)


def home_next_kernel(slot_ref, live_ref, recv_ref, mass_ref, old_ref, send_ref, row_ref, parts_ref):
    home_gather(slot_ref, live_ref, recv_ref, parts_ref, 0.0)
    total = jnp.sum(parts_ref[...], axis=0)
    row_ref[...] = old_ref[...] + jnp.log2(mass_ref[...]) - jnp.log2(total)
    home_scatter(slot_ref, row_ref, send_ref)


def home_last_kernel(slot_ref, live_ref, recv_ref, pos_ref, vel_ref, new_pos_ref, new_vel_ref):
    blocks = live_ref.shape[0]
    for b in range(blocks):
        live = live_ref[b]
        parts = jnp.zeros((ROWS, BLK), f32)
        for k in range(K):
            rows = recv_ref[pl.ds(slot_ref[b * K + k] * ROWS, ROWS), :]
            parts = parts + jnp.where(k < live, rows, 0.0)
        where = slice(b * BLK, (b + 1) * BLK)
        centre = parts[0:3] / parts[3:4] + 0.5
        here = pos_ref[:, where]
        velocity = vel_ref[:, where] + STIFFNESS * (centre - here)
        new_vel_ref[:, where] = velocity
        new_pos_ref[:, where] = here + TIMESTEP * velocity


def sample_kernel(sample_ref, tiles_ref):
    tiles = tiles_ref.shape[0]
    row = lax.broadcasted_iota(jnp.int32, (8, TILE), 0)

    def body(t, carry):
        where = pl.ds(pl.multiple_of(t * TILE, TILE), TILE)
        parts = [jnp.broadcast_to(sample_ref[d : d + 1, where], (8, TILE)) - 0.5 for d in range(3)]
        square = parts[0] * parts[0] + parts[1] * parts[1] + parts[2] * parts[2]
        value = (-0.5 * SCALE) * square
        for d in range(3):
            value = jnp.where((row == d) | (row == d + 5), parts[d], value)
        high, middle, low = split3(value)
        one = row == 3
        first = jnp.where(one, 1.0, jnp.where(row > 4, middle, high))
        second = jnp.where(one, 1.0, jnp.where(row > 4, low, middle))
        third = jnp.where(one, 1.0, jnp.where(row == 4, low, high))
        zero = jnp.zeros_like(first)
        tiles_ref[t] = jnp.concatenate([first, second, third, zero], 0).astype(bf16)
        return carry

    lax.fori_loop(0, tiles, body, 0, unroll=4)


def lanes_of(ref):
    tiles = ref.shape[0] // CHUNKS
    return jnp.concatenate([ref[pl.ds(c, tiles, stride=CHUNKS), :] for c in range(CHUNKS)], 1)


def particle_rows(recv_ref, slot, extra, row):
    parts = [
        (jnp.broadcast_to(recv_ref[pl.ds(slot * ROWS + d, 1), :], (8, BLK)) - 0.5) for d in range(3)
    ]
    square = parts[0] * parts[0] + parts[1] * parts[1] + parts[2] * parts[2]
    value = (-0.5 * SCALE) * square + extra
    for d in range(3):
        value = jnp.where((row == d) | (row == d + 5), SCALE * parts[d], value)
    high, middle, low = split3(value)
    one = row == 4
    first = jnp.where(one, 1.0, jnp.where(row > 4, middle, high))
    second = jnp.where(one, 1.0, jnp.where(row == 3, middle, high))
    third = jnp.where(one, 1.0, jnp.where(row < 3, middle, low))
    zero = jnp.zeros_like(first)
    return jnp.concatenate([first, second, third, zero], 0).T.astype(bf16)


def fold_lanes(value):
    out = value[:, :BLK]
    for c in range(1, CHUNKS):
        out = out + value[:, c * BLK : (c + 1) * BLK]
    return out


def product(left, right):
    return jnp.dot(left, right, preferred_element_type=f32)


def row_first_kernel(tile_ref, recv_ref, tiles_ref, pot_ref, part_ref, list_ref, size_ref, beta_ref, top_ref):
    slots = tile_ref.shape[0]
    tiles = tiles_ref.shape[0]

    def compact(g, count):
        for k in range(G):
            slot = g * G + k
            tile = tile_ref[slot]
            list_ref[0, count] = slot
            list_ref[1, count] = tile
            list_ref[2, count] = tile
            count = count + jnp.where(tile >= 0, 1, 0)
        return count

    count = lax.fori_loop(0, slots // G, compact, 0)
    size_ref[0] = (count + G - 1) // G
    for k in range(G):
        list_ref[0, count + k] = list_ref[0, 0]
        list_ref[1, count + k] = list_ref[1, 0]
        list_ref[2, count + k] = tiles

    pot = lanes_of(pot_ref) * SCALE
    top = jnp.max(pot, axis=1, keepdims=True)
    beta_ref[...] = pot - top
    top_ref[...] = jnp.broadcast_to(top - ROW_SHIFT, top_ref.shape)
    row = lax.broadcasted_iota(jnp.int32, (8, BLK), 0)

    def body(g, carry):
        slot = [list_ref[0, g * G + k] for k in range(G)]
        tile = [list_ref[1, g * G + k] for k in range(G)]
        left = [particle_rows(recv_ref, s, ROW_SHIFT, row) for s in slot]
        raised = [product(a, tiles_ref[t]) for a, t in zip(left, tile)]
        power = [jnp.exp2(a + beta_ref[pl.ds(t, 1), :]) for a, t in zip(raised, tile)]
        total = [jnp.sum(fold_lanes(a).T, axis=0, keepdims=True) for a in power]
        for k in range(G):
            part_ref[pl.ds(slot[k], 1), :] = jnp.log2(total[k]) + top_ref[pl.ds(tile[k], 1), :]
        return carry

    lax.fori_loop(0, size_ref[0], body, 0)


def column_pass(list_ref, groups, recv_ref, rows_ref, tiles_ref, mass_ref, left_ref, sums_ref, peak_ref, pot_ref):
    tiles = tiles_ref.shape[0]
    peak_ref[...] = jnp.full(peak_ref.shape, NEGATIVE, f32)

    def find(g, carry):
        for k in range(G):
            at = pl.ds(list_ref[2, g * G + k], 1)
            peak_ref[at, :] = jnp.maximum(peak_ref[at, :], rows_ref[pl.ds(list_ref[0, g * G + k], 1), :])
        return carry

    lax.fori_loop(0, groups, find, 0)
    peak = jnp.max(peak_ref[0:tiles, :], axis=1, keepdims=True)
    peak_ref[0:tiles, :] = jnp.broadcast_to(COL_SHIFT - peak, (tiles, BLK))
    sums_ref[...] = jnp.zeros(sums_ref.shape, f32)
    row = lax.broadcasted_iota(jnp.int32, (8, BLK), 0)

    def body(g, carry):
        slot = [list_ref[0, g * G + k] for k in range(G)]
        tile = [list_ref[1, g * G + k] for k in range(G)]
        into = [list_ref[2, g * G + k] for k in range(G)]
        extra = [
            jnp.broadcast_to(rows_ref[pl.ds(s, 1), :] + peak_ref[pl.ds(t, 1), :], (8, BLK))
            for s, t in zip(slot, tile)
        ]
        left = [particle_rows(recv_ref, s, e, row) for s, e in zip(slot, extra)]
        for k in range(G):
            left_ref[g * G + k] = left[k]
        raised = [product(a, tiles_ref[t]) for a, t in zip(left, tile)]
        total = [jnp.sum(jnp.exp2(a).reshape(BLK // 8, 8, TILE), axis=0) for a in raised]
        for k in range(G):
            sums_ref[into[k]] += total[k]
        return carry

    lax.fori_loop(0, groups, body, 0)
    total = jnp.sum(sums_ref[0:tiles], axis=1)
    pot_ref[...] = jnp.log2(lanes_of(mass_ref)) - jnp.log2(total)


def middle_kernel(list_ref, size_ref, recv_ref, rows_ref, tiles_ref, mass_ref, part_ref, left_ref, sums_ref, peak_ref, pot_ref):
    groups = size_ref[0]
    column_pass(list_ref, groups, recv_ref, rows_ref, tiles_ref, mass_ref, left_ref, sums_ref, peak_ref, pot_ref)

    def body(g, carry):
        slot = [list_ref[0, g * G + k] for k in range(G)]
        tile = [list_ref[1, g * G + k] for k in range(G)]
        raised = [product(left_ref[g * G + k], tiles_ref[tile[k]]) for k in range(G)]
        power = [jnp.exp2(a + pot_ref[pl.ds(t, 1), :]) for a, t in zip(raised, tile)]
        total = [jnp.sum(fold_lanes(a).T, axis=0, keepdims=True) for a in power]
        for k in range(G):
            part_ref[pl.ds(slot[k], 1), :] = total[k]
        return carry

    lax.fori_loop(0, groups, body, 0)


def last_kernel(list_ref, size_ref, recv_ref, rows_ref, tiles_ref, mass_ref, sample_ref, part_ref, left_ref, sums_ref, peak_ref, pot_ref):
    groups = size_ref[0]
    column_pass(list_ref, groups, recv_ref, rows_ref, tiles_ref, mass_ref, left_ref, sums_ref, peak_ref, pot_ref)
    pieces = 2

    def body(h, carry):
        for j in range(G // pieces):
            at = [h * G + j * pieces + k for k in range(pieces)]
            slot = [list_ref[0, i] for i in at]
            tile = [list_ref[1, i] for i in at]
            raised = [product(left_ref[i], tiles_ref[t]) for i, t in zip(at, tile)]
            power = [jnp.exp2(a + pot_ref[pl.ds(t, 1), :]) for a, t in zip(raised, tile)]
            for k in range(pieces):
                where = pl.ds(pl.multiple_of(tile[k] * TILE, TILE), TILE)
                for d in range(3):
                    place = sample_ref[d : d + 1, where] - 0.5
                    part_ref[pl.ds(slot[k] * ROWS + d, 1), :] = jnp.sum(
                        fold_lanes(power[k] * place).T, axis=0, keepdims=True
                    )
                part_ref[pl.ds(slot[k] * ROWS + 3, 1), :] = jnp.sum(
                    fold_lanes(power[k]).T, axis=0, keepdims=True
                )
        return carry

    lax.fori_loop(0, groups, body, 0)


def local(
    positions,
    velocities,
    masses,
    samples,
    sample_mass,
    start_potential,
    route_owner,
    route_tile,
    live_count,
):
    devices = lax.axis_size("dev")
    blocks = route_owner.shape[0]
    tiles = start_potential.shape[0] // TILE
    capacity = 2 * blocks * K // devices
    slots = devices * capacity
    struct = jax.ShapeDtypeStruct

    def exchange(values):
        rows = values.shape[0] // devices
        got = lax.all_to_all(
            values.reshape(devices, rows, BLK), "dev", split_axis=0, concat_axis=0, tiled=True
        )
        return got.reshape(values.shape)

    send, slot = call(
        functools.partial(setup_kernel, capacity),
        (struct((slots * ROWS, BLK), f32), struct((blocks * K,), jnp.int32)),
        [SMEM, SMEM, SMEM, VMEM],
        (VMEM, SMEM),
        [pltpu.SMEM((devices,), jnp.int32)],
        10**6,
        (route_owner, route_tile, live_count, positions),
    )
    recv = exchange(send)
    split_tiles = call(
        sample_kernel,
        struct((tiles, DEPTH, TILE), bf16),
        [VMEM],
        VMEM,
        [],
        10**7,
        (samples,),
    )
    mass_rows = masses.reshape(blocks, BLK)
    sample_rows = sample_mass.reshape(tiles * CHUNKS, BLK)
    pot_rows = start_potential.reshape(tiles * CHUNKS, BLK)
    asked = recv.reshape(slots, ROWS, BLK)[:, 3, 0].astype(jnp.int32)

    part, listed, size = call(
        row_first_kernel,
        (struct((slots, BLK), f32), struct((3, slots + 2 * G), jnp.int32), struct((1,), jnp.int32)),
        [SMEM, VMEM, VMEM, VMEM],
        (VMEM, SMEM, SMEM),
        [pltpu.VMEM((tiles, TILE), f32), pltpu.VMEM((tiles, BLK), f32)],
        10**9,
        (asked, recv, split_tiles, pot_rows),
    )
    part = exchange(part)
    row_scratch = [pltpu.VMEM((K, blocks, BLK), f32)]
    row_out = (struct((slots, BLK), f32), struct((blocks, BLK), f32))
    send, row = call(
        home_first_kernel,
        row_out,
        [SMEM, SMEM, VMEM, VMEM],
        (VMEM, VMEM),
        row_scratch,
        10**6,
        (slot, live_count, part, mass_rows),
    )
    rows = exchange(send)
    scratch = [
        pltpu.VMEM((slots + G, BLK, DEPTH), bf16),
        pltpu.VMEM((tiles + 1, 8, TILE), f32),
        pltpu.VMEM((tiles + 8, BLK), f32),
        pltpu.VMEM((tiles, TILE), f32),
    ]
    part = call(
        middle_kernel,
        struct((slots, BLK), f32),
        [SMEM, SMEM] + [VMEM] * 4,
        VMEM,
        scratch,
        10**9,
        (listed, size, recv, rows, split_tiles, sample_rows),
    )
    part = exchange(part)
    send, row = call(
        home_next_kernel,
        row_out,
        [SMEM, SMEM, VMEM, VMEM, VMEM],
        (VMEM, VMEM),
        row_scratch,
        10**6,
        (slot, live_count, part, mass_rows, row),
    )
    rows = exchange(send)
    part = call(
        last_kernel,
        struct((slots * ROWS, BLK), f32),
        [SMEM, SMEM] + [VMEM] * 5,
        VMEM,
        scratch,
        10**9,
        (listed, size, recv, rows, split_tiles, sample_rows, samples),
    )
    part = exchange(part)
    return call(
        home_last_kernel,
        (struct(positions.shape, f32), struct(positions.shape, f32)),
        [SMEM, SMEM, VMEM, VMEM, VMEM],
        (VMEM, VMEM),
        [],
        10**6,
        (slot, live_count, part, positions, velocities),
    )


def solution(mesh):
    placed = (
        P(None, "dev"),
        P(None, "dev"),
        P("dev"),
        P(None, "dev"),
        P("dev"),
        P("dev"),
        P("dev", None),
        P("dev", None),
        P("dev"),
    )
    return jax.shard_map(
        local,
        mesh=mesh,
        in_specs=placed,
        out_specs=(P(None, "dev"), P(None, "dev")),
        check_vma=False,
    )
```

```python
import functools
import jax
import jax.numpy as jnp
from jax import lax
from jax.experimental import pallas as pl
from jax.experimental.pallas import tpu as pltpu
from jax.sharding import PartitionSpec as P

BLK = 128
TILE = 512
K = 4
CHUNKS = TILE // BLK
EPSILON = 0.01
STIFFNESS = 150.0
TIMESTEP = 0.05
LOG2E = 1.4426950408889634
SCALE = LOG2E / EPSILON
NEGATIVE = -1e30
ROW_SHIFT = 115.0
COL_SHIFT = 110.0
G = 16
KEPT = 208
ROWS = 4
DEPTH = 32

f32 = jnp.float32
bf16 = jnp.bfloat16
VMEM = pl.BlockSpec(memory_space=pltpu.VMEM)
SMEM = pl.BlockSpec(memory_space=pltpu.SMEM)


def call(kernel, out_shape, in_specs, out_specs, scratch, flops, args):
    size = sum(a.size * a.dtype.itemsize for a in args)
    return pl.pallas_call(
        kernel,
        out_shape=out_shape,
        in_specs=in_specs,
        out_specs=out_specs,
        scratch_shapes=scratch,
        compiler_params=pltpu.CompilerParams(vmem_limit_bytes=67_000_000),
        cost_estimate=pl.CostEstimate(flops=flops, bytes_accessed=size, transcendentals=0),
    )(*args)


def split3(value):
    high = value.astype(bf16).astype(f32)
    rest = value - high
    middle = rest.astype(bf16).astype(f32)
    return high, middle, rest - middle


def setup_kernel(capacity, owner_ref, tile_ref, live_ref, pos_ref, send_ref, slot_ref, count_ref):
    blocks = live_ref.shape[0]
    stride = capacity * ROWS

    def clear(i, carry):
        count_ref[i] = 0
        return carry

    lax.fori_loop(0, count_ref.shape[0], clear, 0)
    send_ref[...] = jnp.full(send_ref.shape, -1.0, f32)
    for b in range(blocks):
        rows = [pos_ref[d : d + 1, b * BLK : (b + 1) * BLK] for d in range(3)]
        for k in range(K):
            owner = owner_ref[k, b]
            rank = count_ref[owner]
            count_ref[owner] = rank + 1
            slot_ref[b * K + k] = owner * capacity + rank
            tile = jnp.where(k < live_ref[b], tile_ref[k, b], -1).astype(f32)
            base = owner * stride + rank
            for d in range(3):
                send_ref[pl.ds(base + d * capacity, 1), :] = rows[d]
            send_ref[pl.ds(base + 3 * capacity, 1), :] = jnp.full((1, BLK), tile, f32)


def home_gather(slot_ref, live_ref, recv_ref, parts_ref, filler):
    blocks = live_ref.shape[0]
    for b in range(blocks):
        live = live_ref[b]
        for k in range(K):
            row = recv_ref[pl.ds(slot_ref[b * K + k], 1), :]
            parts_ref[k, b : b + 1, :] = jnp.where(k < live, row, filler)


def home_scatter(slot_ref, rows_ref, send_ref):
    for b in range(rows_ref.shape[0]):
        row = rows_ref[b : b + 1, :]
        for k in range(K):
            send_ref[pl.ds(slot_ref[b * K + k], 1), :] = row


def home_first_kernel(slot_ref, live_ref, recv_ref, mass_ref, send_ref, row_ref, parts_ref):
    home_gather(slot_ref, live_ref, recv_ref, parts_ref, NEGATIVE)
    parts = parts_ref[...]
    top = jnp.max(parts, axis=0)
    total = jnp.sum(jnp.exp2(parts - top[None]), axis=0)
    row_ref[...] = jnp.log2(mass_ref[...]) - (top + jnp.log2(total))
    home_scatter(slot_ref, row_ref, send_ref)


def home_next_kernel(slot_ref, live_ref, recv_ref, mass_ref, old_ref, send_ref, row_ref, parts_ref):
    home_gather(slot_ref, live_ref, recv_ref, parts_ref, 0.0)
    total = jnp.sum(parts_ref[...], axis=0)
    row_ref[...] = old_ref[...] + jnp.log2(mass_ref[...]) - jnp.log2(total)
    home_scatter(slot_ref, row_ref, send_ref)


def home_last_kernel(slot_ref, live_ref, recv_ref, pos_ref, vel_ref, new_pos_ref, new_vel_ref):
    blocks = live_ref.shape[0]
    for b in range(blocks):
        live = live_ref[b]
        parts = jnp.zeros((ROWS, BLK), f32)
        for k in range(K):
            rows = recv_ref[pl.ds(slot_ref[b * K + k] * ROWS, ROWS), :]
            parts = parts + jnp.where(k < live, rows, 0.0)
        where = slice(b * BLK, (b + 1) * BLK)
        centre = parts[0:3] / parts[3:4] + 0.5
        here = pos_ref[:, where]
        velocity = vel_ref[:, where] + STIFFNESS * (centre - here)
        new_vel_ref[:, where] = velocity
        new_pos_ref[:, where] = here + TIMESTEP * velocity


def sample_kernel(sample_ref, tiles_ref):
    tiles = tiles_ref.shape[0]
    row = lax.broadcasted_iota(jnp.int32, (8, TILE), 0)

    def body(t, carry):
        where = pl.ds(pl.multiple_of(t * TILE, TILE), TILE)
        parts = [jnp.broadcast_to(sample_ref[d : d + 1, where], (8, TILE)) - 0.5 for d in range(3)]
        square = parts[0] * parts[0] + parts[1] * parts[1] + parts[2] * parts[2]
        value = (-0.5 * SCALE) * square
        for d in range(3):
            value = jnp.where((row == d) | (row == d + 5), parts[d], value)
        high, middle, low = split3(value)
        one = row == 3
        first = jnp.where(one, 1.0, jnp.where(row > 4, middle, high))
        second = jnp.where(one, 1.0, jnp.where(row > 4, low, middle))
        third = jnp.where(one, 1.0, jnp.where(row == 4, low, high))
        zero = jnp.zeros_like(first)
        tiles_ref[t] = jnp.concatenate([first, second, third, zero], 0).astype(bf16)
        return carry

    lax.fori_loop(0, tiles, body, 0, unroll=4)


def lanes_of(ref):
    tiles = ref.shape[0] // CHUNKS
    return jnp.concatenate([ref[pl.ds(c, tiles, stride=CHUNKS), :] for c in range(CHUNKS)], 1)


def particle_rows(recv_ref, place, extra, row):
    base, capacity = place
    parts = [
        (jnp.broadcast_to(recv_ref[pl.ds(base + d * capacity, 1), :], (8, BLK)) - 0.5)
        for d in range(3)
    ]
    square = parts[0] * parts[0] + parts[1] * parts[1] + parts[2] * parts[2]
    value = (-0.5 * SCALE) * square + extra
    for d in range(3):
        value = jnp.where((row == d) | (row == d + 5), SCALE * parts[d], value)
    high, middle, low = split3(value)
    one = row == 4
    first = jnp.where(one, 1.0, jnp.where(row > 4, middle, high))
    second = jnp.where(one, 1.0, jnp.where(row == 3, middle, high))
    third = jnp.where(one, 1.0, jnp.where(row < 3, middle, low))
    zero = jnp.zeros_like(first)
    return jnp.concatenate([first, second, third, zero], 0).T.astype(bf16)


def fold_lanes(value):
    out = value[:, :BLK]
    for c in range(1, CHUNKS):
        out = out + value[:, c * BLK : (c + 1) * BLK]
    return out


def product(left, right):
    return jnp.dot(left, right, preferred_element_type=f32)


def row_first_kernel(
    capacity,
    recv_ref,
    tiles_ref,
    pot_ref,
    part_ref,
    list_ref,
    size_ref,
    beta_ref,
    top_ref,
    asked_ref,
    tile_ref,
    sem,
):
    devices = asked_ref.shape[0]
    lane = lax.broadcasted_iota(jnp.int32, (devices, capacity, BLK), 2)
    rank = lax.broadcasted_iota(jnp.int32, (devices, capacity, BLK), 1)
    asked = recv_ref[...].reshape(devices, ROWS * capacity, BLK)[:, 3 * capacity :, :]
    asked_ref[...] = jnp.sum(jnp.where(lane == rank, asked, 0.0), axis=1).astype(jnp.int32)
    copy = pltpu.make_async_copy(asked_ref, tile_ref, sem)
    copy.start()

    pot = lanes_of(pot_ref) * SCALE
    top = jnp.max(pot, axis=1, keepdims=True)
    beta_ref[...] = pot - top
    top_ref[...] = jnp.broadcast_to(top - ROW_SHIFT, top_ref.shape)
    row = lax.broadcasted_iota(jnp.int32, (8, BLK), 0)
    copy.wait()

    def compact(device, count):
        for k in range(capacity):
            tile = tile_ref[device, k]
            list_ref[0, count] = device * capacity + k
            list_ref[1, count] = tile
            list_ref[2, count] = device * (capacity * ROWS) + k
            count = count + jnp.where(tile >= 0, 1, 0)
        return count

    count = lax.fori_loop(0, devices, compact, 0)
    size_ref[0] = (count + G - 1) // G
    size_ref[1] = count
    for k in range(G):
        for i in range(3):
            list_ref[i, count + k] = list_ref[i, 0]

    def body(g, carry):
        slot = [list_ref[0, g * G + k] for k in range(G)]
        tile = [list_ref[1, g * G + k] for k in range(G)]
        base = [list_ref[2, g * G + k] for k in range(G)]
        left = [particle_rows(recv_ref, (i, capacity), ROW_SHIFT, row) for i in base]
        raised = [product(a, tiles_ref[t]) for a, t in zip(left, tile)]
        power = [jnp.exp2(a + beta_ref[pl.ds(t, 1), :]) for a, t in zip(raised, tile)]
        total = [jnp.sum(fold_lanes(a).T, axis=0, keepdims=True) for a in power]
        for k in range(G):
            part_ref[pl.ds(slot[k], 1), :] = jnp.log2(total[k]) + top_ref[pl.ds(tile[k], 1), :]
        return carry

    lax.fori_loop(0, size_ref[0], body, 0)


def iterate(
    capacity,
    weights,
    store,
    list_ref,
    size_ref,
    recv_ref,
    rows_ref,
    tiles_ref,
    mass_ref,
    kept_ref,
    sums_ref,
    peak_ref,
    weight_ref,
):
    tiles = tiles_ref.shape[0]
    groups, count = size_ref[0], size_ref[1]
    limit = jnp.minimum(groups, KEPT // G)
    row = lax.broadcasted_iota(jnp.int32, (8, BLK), 0)
    peak_ref[...] = jnp.full(peak_ref.shape, NEGATIVE, f32)

    def find(g, carry):
        for k in range(G):
            at = pl.ds(list_ref[1, g * G + k], 1)
            peak_ref[at, :] = jnp.maximum(
                peak_ref[at, :], rows_ref[pl.ds(list_ref[0, g * G + k], 1), :]
            )
        return carry

    lax.fori_loop(0, groups, find, 0)
    peak = jnp.max(peak_ref[...], axis=1, keepdims=True)
    peak_ref[...] = jnp.broadcast_to(COL_SHIFT - peak, peak_ref.shape)
    sums_ref[...] = jnp.zeros(sums_ref.shape, f32)

    def powers(g):
        slot = [list_ref[0, g * G + k] for k in range(G)]
        tile = [list_ref[1, g * G + k] for k in range(G)]
        base = [list_ref[2, g * G + k] for k in range(G)]
        extra = [
            jnp.broadcast_to(rows_ref[pl.ds(s, 1), :] + peak_ref[pl.ds(t, 1), :], (8, BLK))
            for s, t in zip(slot, tile)
        ]
        left = [particle_rows(recv_ref, (i, capacity), e, row) for i, e in zip(base, extra)]
        raised = [product(a, tiles_ref[t]) for a, t in zip(left, tile)]
        return slot, tile, [jnp.exp2(a) for a in raised]

    def add_up(g, tile, power):
        total = [jnp.sum(a.reshape(BLK // 8, 8, TILE), axis=0) for a in power]
        for k in range(G):
            into = jnp.where(g * G + k < count, tile[k], tiles)
            sums_ref[into] += total[k]

    def first_kept(g, carry):
        slot, tile, power = powers(g)
        for k in range(G):
            kept_ref[g * G + k] = power[k]
        add_up(g, tile, power)
        return carry

    def first_rest(g, carry):
        slot, tile, power = powers(g)
        add_up(g, tile, power)
        return carry

    lax.fori_loop(0, limit, first_kept, 0)
    lax.fori_loop(limit, groups, first_rest, 0)
    total = jnp.sum(sums_ref[0:tiles], axis=1)
    weights(lanes_of(mass_ref) / total, weight_ref)

    def second_kept(g, carry):
        for k in range(G):
            store(list_ref[0, g * G + k], list_ref[1, g * G + k], kept_ref[g * G + k], weight_ref)
        return carry

    def second_rest(g, carry):
        slot, tile, power = powers(g)
        for k in range(G):
            store(slot[k], tile[k], power[k], weight_ref)
        return carry

    lax.fori_loop(0, limit, second_kept, 0)
    lax.fori_loop(limit, groups, second_rest, 0)


def middle_kernel(
    capacity, list_ref, size_ref, recv_ref, rows_ref, tiles_ref, mass_ref, part_ref, *scratch
):
    def weights(value, weight_ref):
        weight_ref[...] = value

    def store(slot, tile, power, weight_ref):
        power = power * weight_ref[pl.ds(tile, 1), :]
        part_ref[pl.ds(slot, 1), :] = jnp.sum(fold_lanes(power).T, axis=0, keepdims=True)

    iterate(
        capacity,
        weights,
        store,
        list_ref,
        size_ref,
        recv_ref,
        rows_ref,
        tiles_ref,
        mass_ref,
        *scratch,
    )


def last_kernel(
    capacity,
    list_ref,
    size_ref,
    recv_ref,
    rows_ref,
    tiles_ref,
    mass_ref,
    sample_ref,
    part_ref,
    *scratch,
):
    *scratch, value_ref = scratch
    row = lax.broadcasted_iota(jnp.int32, (8, TILE), 0)

    def weights(value, weight_ref):
        value_ref[...] = value

        def body(t, carry):
            where = pl.ds(pl.multiple_of(t * TILE, TILE), TILE)
            place = jnp.ones((8, TILE), f32)
            for d in range(3):
                part = jnp.broadcast_to(sample_ref[d : d + 1, where], (8, TILE)) - 0.5
                place = jnp.where((row == d) | (row == d + 4), part, place)
            high, middle, low = split3(place * value_ref[pl.ds(t, 1), :])
            upper = jnp.where(row < 4, high, middle)
            lower = jnp.where(row < 4, low, 0.0)
            weight_ref[t] = jnp.concatenate([upper, lower], 0).astype(bf16)
            return carry

        lax.fori_loop(0, value_ref.shape[0], body, 0, unroll=4)

    def store(slot, tile, power, weight_ref):
        left = weight_ref[tile]
        high = power.astype(bf16)
        low = (power - high.astype(f32)).astype(bf16)
        dims = (((1,), (1,)), ((), ()))
        out = lax.dot_general(left, high, dims, preferred_element_type=f32)
        out = out + lax.dot_general(left, low, dims, preferred_element_type=f32)
        out = out[0:8] + out[8:16]
        part_ref[pl.ds(pl.multiple_of(slot * ROWS, ROWS), ROWS), :] = out[0:4] + out[4:8]

    iterate(
        capacity,
        weights,
        store,
        list_ref,
        size_ref,
        recv_ref,
        rows_ref,
        tiles_ref,
        mass_ref,
        *scratch,
    )


def local(
    positions,
    velocities,
    masses,
    samples,
    sample_mass,
    start_potential,
    route_owner,
    route_tile,
    live_count,
):
    devices = lax.axis_size("dev")
    blocks = route_owner.shape[0]
    tiles = start_potential.shape[0] // TILE
    capacity = 2 * blocks * K // devices
    slots = devices * capacity
    struct = jax.ShapeDtypeStruct

    def exchange(values):
        rows = values.shape[0] // devices
        got = lax.all_to_all(
            values.reshape(devices, rows, BLK), "dev", split_axis=0, concat_axis=0, tiled=True
        )
        return got.reshape(values.shape)

    send, slot = call(
        functools.partial(setup_kernel, capacity),
        (struct((slots * ROWS, BLK), f32), struct((blocks * K,), jnp.int32)),
        [SMEM, SMEM, SMEM, VMEM],
        (VMEM, SMEM),
        [pltpu.SMEM((devices,), jnp.int32)],
        10**6,
        (route_owner.T, route_tile.T, live_count, positions),
    )
    recv = exchange(send)
    split_tiles = call(
        sample_kernel,
        struct((tiles, DEPTH, TILE), bf16),
        [VMEM],
        VMEM,
        [],
        10**7,
        (samples,),
    )
    mass_rows = masses.reshape(blocks, BLK)
    sample_rows = sample_mass.reshape(tiles * CHUNKS, BLK)
    pot_rows = start_potential.reshape(tiles * CHUNKS, BLK)
    part, listed, size = call(
        functools.partial(row_first_kernel, capacity),
        (struct((slots, BLK), f32), struct((3, slots + 2 * G), jnp.int32), struct((2,), jnp.int32)),
        [VMEM, VMEM, VMEM],
        (VMEM, SMEM, SMEM),
        [
            pltpu.VMEM((tiles, TILE), f32),
            pltpu.VMEM((tiles, BLK), f32),
            pltpu.VMEM((devices, BLK), jnp.int32),
            pltpu.SMEM((devices, BLK), jnp.int32),
            pltpu.SemaphoreType.DMA,
        ],
        10**9,
        (recv, split_tiles, pot_rows),
    )
    part = exchange(part)
    row_scratch = [pltpu.VMEM((K, blocks, BLK), f32)]
    row_out = (struct((slots, BLK), f32), struct((blocks, BLK), f32))
    send, row = call(
        home_first_kernel,
        row_out,
        [SMEM, SMEM, VMEM, VMEM],
        (VMEM, VMEM),
        row_scratch,
        10**6,
        (slot, live_count, part, mass_rows),
    )
    rows = exchange(send)
    scratch = [
        pltpu.VMEM((min(KEPT, slots), BLK, TILE), f32),
        pltpu.VMEM((tiles + 1, 8, TILE), f32),
        pltpu.VMEM((tiles, BLK), f32),
    ]
    values = pltpu.VMEM((tiles, TILE), f32)
    part = call(
        functools.partial(middle_kernel, capacity),
        struct((slots, BLK), f32),
        [SMEM, SMEM] + [VMEM] * 4,
        VMEM,
        scratch + [values],
        10**9,
        (listed, size, recv, rows, split_tiles, sample_rows),
    )
    part = exchange(part)
    send, row = call(
        home_next_kernel,
        row_out,
        [SMEM, SMEM, VMEM, VMEM, VMEM],
        (VMEM, VMEM),
        row_scratch,
        10**6,
        (slot, live_count, part, mass_rows, row),
    )
    rows = exchange(send)
    part = call(
        functools.partial(last_kernel, capacity),
        struct((slots * ROWS, BLK), f32),
        [SMEM, SMEM] + [VMEM] * 5,
        VMEM,
        scratch + [pltpu.VMEM((tiles, 16, TILE), bf16), values],
        10**9,
        (listed, size, recv, rows, split_tiles, sample_rows, samples),
    )
    part = exchange(part)
    return call(
        home_last_kernel,
        (struct(positions.shape, f32), struct(positions.shape, f32)),
        [SMEM, SMEM, VMEM, VMEM, VMEM],
        (VMEM, VMEM),
        [],
        10**6,
        (slot, live_count, part, positions, velocities),
    )


def solution(mesh):
    placed = (
        P(None, "dev"),
        P(None, "dev"),
        P("dev"),
        P(None, "dev"),
        P("dev"),
        P("dev"),
        P("dev", None),
        P("dev", None),
        P("dev"),
    )
    return jax.shard_map(
        local,
        mesh=mesh,
        in_specs=placed,
        out_specs=(P(None, "dev"), P(None, "dev")),
        check_vma=False,
    )
```

```python
import functools
import jax
import jax.numpy as jnp
from jax import lax
from jax.experimental import pallas as pl
from jax.experimental.pallas import tpu as pltpu
from jax.sharding import PartitionSpec as P

BLK = 128
TILE = 512
K = 4
CHUNKS = TILE // BLK
EPSILON = 0.01
STIFFNESS = 150.0
TIMESTEP = 0.05
LOG2E = 1.4426950408889634
SCALE = LOG2E / EPSILON
NEGATIVE = -1e30
ROW_SHIFT = 115.0
COL_SHIFT = 110.0
G = 16
KEPT = 208
ROWS = 4
DEPTH = 32

f32 = jnp.float32
bf16 = jnp.bfloat16
VMEM = pl.BlockSpec(memory_space=pltpu.VMEM)
ANY = pl.BlockSpec(memory_space=pl.ANY)
SMEM = pl.BlockSpec(memory_space=pltpu.SMEM)


def call(kernel, out_shape, in_specs, out_specs, scratch, flops, args):
    size = sum(a.size * a.dtype.itemsize for a in args)
    return pl.pallas_call(
        kernel,
        out_shape=out_shape,
        in_specs=in_specs,
        out_specs=out_specs,
        scratch_shapes=scratch,
        compiler_params=pltpu.CompilerParams(vmem_limit_bytes=67_000_000),
        cost_estimate=pl.CostEstimate(flops=flops, bytes_accessed=size, transcendentals=0),
    )(*args)


def split3(value):
    high = value.astype(bf16).astype(f32)
    rest = value - high
    middle = rest.astype(bf16).astype(f32)
    return high, middle, rest - middle


def setup_kernel(capacity, owner_ref, tile_ref, live_ref, pos_ref, send_ref, slot_ref, count_ref):
    blocks = live_ref.shape[0]
    stride = capacity * ROWS

    def clear(i, carry):
        count_ref[i] = 0
        return carry

    lax.fori_loop(0, count_ref.shape[0], clear, 0)
    send_ref[...] = jnp.full(send_ref.shape, -1.0, f32)
    for b in range(blocks):
        rows = [pos_ref[d : d + 1, b * BLK : (b + 1) * BLK] for d in range(3)]
        for k in range(K):
            owner = owner_ref[k, b]
            rank = count_ref[owner]
            count_ref[owner] = rank + 1
            slot_ref[b * K + k] = owner * capacity + rank
            tile = jnp.where(k < live_ref[b], tile_ref[k, b], -1).astype(f32)
            base = owner * stride + rank
            for d in range(3):
                send_ref[pl.ds(base + d * capacity, 1), :] = rows[d]
            send_ref[pl.ds(base + 3 * capacity, 1), :] = jnp.full((1, BLK), tile, f32)


def home_gather(slot_ref, live_ref, recv_ref, parts_ref, filler):
    blocks = live_ref.shape[0]
    for b in range(blocks):
        live = live_ref[b]
        for k in range(K):
            row = recv_ref[pl.ds(slot_ref[b * K + k], 1), :]
            parts_ref[k, b : b + 1, :] = jnp.where(k < live, row, filler)


def home_scatter(slot_ref, rows_ref, send_ref):
    for b in range(rows_ref.shape[0]):
        row = rows_ref[b : b + 1, :]
        for k in range(K):
            send_ref[pl.ds(slot_ref[b * K + k], 1), :] = row


def home_first_kernel(slot_ref, live_ref, recv_ref, mass_ref, send_ref, row_ref, parts_ref):
    home_gather(slot_ref, live_ref, recv_ref, parts_ref, NEGATIVE)
    parts = parts_ref[...]
    top = jnp.max(parts, axis=0)
    total = jnp.sum(jnp.exp2(parts - top[None]), axis=0)
    row_ref[...] = jnp.log2(mass_ref[...]) - (top + jnp.log2(total))
    home_scatter(slot_ref, row_ref, send_ref)


def home_next_kernel(slot_ref, live_ref, recv_ref, mass_ref, old_ref, send_ref, row_ref, parts_ref):
    home_gather(slot_ref, live_ref, recv_ref, parts_ref, 0.0)
    total = jnp.sum(parts_ref[...], axis=0)
    row_ref[...] = old_ref[...] + jnp.log2(mass_ref[...]) - jnp.log2(total)
    home_scatter(slot_ref, row_ref, send_ref)


def home_last_kernel(slot_ref, live_ref, recv_ref, pos_ref, vel_ref, new_pos_ref, new_vel_ref):
    blocks = live_ref.shape[0]
    for b in range(blocks):
        live = live_ref[b]
        parts = jnp.zeros((ROWS, BLK), f32)
        for k in range(K):
            rows = recv_ref[pl.ds(slot_ref[b * K + k] * ROWS, ROWS), :]
            parts = parts + jnp.where(k < live, rows, 0.0)
        where = slice(b * BLK, (b + 1) * BLK)
        centre = parts[0:3] / parts[3:4] + 0.5
        here = pos_ref[:, where]
        velocity = vel_ref[:, where] + STIFFNESS * (centre - here)
        new_vel_ref[:, where] = velocity
        new_pos_ref[:, where] = here + TIMESTEP * velocity


def sample_kernel(sample_ref, tiles_ref):
    tiles = tiles_ref.shape[0]
    row = lax.broadcasted_iota(jnp.int32, (8, TILE), 0)

    def body(t, carry):
        where = pl.ds(pl.multiple_of(t * TILE, TILE), TILE)
        parts = [jnp.broadcast_to(sample_ref[d : d + 1, where], (8, TILE)) - 0.5 for d in range(3)]
        square = parts[0] * parts[0] + parts[1] * parts[1] + parts[2] * parts[2]
        value = (-0.5 * SCALE) * square
        for d in range(3):
            value = jnp.where((row == d) | (row == d + 5), parts[d], value)
        high, middle, low = split3(value)
        one = row == 3
        first = jnp.where(one, 1.0, jnp.where(row > 4, middle, high))
        second = jnp.where(one, 1.0, jnp.where(row > 4, low, middle))
        third = jnp.where(one, 1.0, jnp.where(row == 4, low, high))
        zero = jnp.zeros_like(first)
        tiles_ref[t] = jnp.concatenate([first, second, third, zero], 0).astype(bf16)
        return carry

    lax.fori_loop(0, tiles, body, 0, unroll=4)


def lanes_of(ref):
    tiles = ref.shape[0] // CHUNKS
    return jnp.concatenate([ref[pl.ds(c, tiles, stride=CHUNKS), :] for c in range(CHUNKS)], 1)


def particle_rows(recv_ref, place, extra, row):
    base, capacity = place
    parts = [
        (jnp.broadcast_to(recv_ref[pl.ds(base + d * capacity, 1), :], (8, BLK)) - 0.5)
        for d in range(3)
    ]
    square = parts[0] * parts[0] + parts[1] * parts[1] + parts[2] * parts[2]
    value = (-0.5 * SCALE) * square + extra
    for d in range(3):
        value = jnp.where((row == d) | (row == d + 5), SCALE * parts[d], value)
    high, middle, low = split3(value)
    one = row == 4
    first = jnp.where(one, 1.0, jnp.where(row > 4, middle, high))
    second = jnp.where(one, 1.0, jnp.where(row == 3, middle, high))
    third = jnp.where(one, 1.0, jnp.where(row < 3, middle, low))
    zero = jnp.zeros_like(first)
    return jnp.concatenate([first, second, third, zero], 0).astype(bf16).T


def fold_lanes(value):
    out = value[:, :BLK]
    for c in range(1, CHUNKS):
        out = out + value[:, c * BLK : (c + 1) * BLK]
    return out


def product(left, right):
    return jnp.dot(left, right, preferred_element_type=f32)


def unpack(list_ref, index, capacity):
    code = list_ref[index]
    slot = lax.shift_right_logical(code, 16)
    device = lax.div(slot, capacity)
    return slot, code & 0xFFFF, slot + device * (capacity * (ROWS - 1))


def listed(list_ref, g, capacity):
    slots = [unpack(list_ref, g * G + k, capacity) for k in range(G)]
    return [list(item) for item in zip(*slots)]


def row_first_kernel(
    capacity,
    recv_ref,
    tiles_any,
    pot_ref,
    part_ref,
    list_ref,
    size_ref,
    tiles_ref,
    beta_ref,
    top_ref,
    left_ref,
    asked_ref,
    tile_ref,
    sems,
):
    load = pltpu.make_async_copy(tiles_any, tiles_ref, sems.at[0])
    load.start()
    devices = asked_ref.shape[0]
    lane = lax.broadcasted_iota(jnp.int32, (devices, capacity, BLK), 2)
    rank = lax.broadcasted_iota(jnp.int32, (devices, capacity, BLK), 1)
    asked = recv_ref[...].reshape(devices, ROWS * capacity, BLK)[:, 3 * capacity :, :]
    asked_ref[...] = jnp.sum(jnp.where(lane == rank, asked, 0.0), axis=1).astype(jnp.int32)
    copy = pltpu.make_async_copy(asked_ref, tile_ref, sems.at[1])
    copy.start()

    pot = lanes_of(pot_ref) * SCALE
    top = jnp.max(pot, axis=1, keepdims=True)
    beta_ref[...] = pot - top
    top_ref[...] = jnp.broadcast_to(top - ROW_SHIFT, top_ref.shape)
    row = lax.broadcasted_iota(jnp.int32, (8, BLK), 0)
    copy.wait()

    def compact(device, count):
        for k in range(capacity):
            tile = tile_ref[device, k]
            list_ref[count] = ((device * capacity + k) << 16) + jnp.maximum(tile, 0)
            count = count + jnp.where(tile >= 0, 1, 0)
        return count

    count = lax.fori_loop(0, devices, compact, 0)
    groups = (count + G - 1) // G
    size_ref[0] = groups
    size_ref[1] = count
    for k in range(G):
        list_ref[count + k] = list_ref[0]

    def prepare(g):
        slot, tile, base = listed(list_ref, g, capacity)
        for k in range(G):
            left_ref[k] = particle_rows(recv_ref, (base[k], capacity), ROW_SHIFT, row)

    prepare(0)
    load.wait()

    def body(g, carry):
        slot, tile, base = listed(list_ref, g, capacity)
        raised = [product(left_ref[k], tiles_ref[tile[k]]) for k in range(G)]
        power = [jnp.exp2(a + beta_ref[pl.ds(t, 1), :]) for a, t in zip(raised, tile)]
        prepare(jnp.minimum(g + 1, groups - 1))
        total = [jnp.sum(fold_lanes(a).T, axis=0, keepdims=True) for a in power]
        for k in range(G):
            part_ref[pl.ds(slot[k], 1), :] = jnp.log2(total[k]) + top_ref[pl.ds(tile[k], 1), :]
        return carry

    lax.fori_loop(0, groups, body, 0)


def iterate(
    capacity,
    weights,
    store,
    list_ref,
    size_ref,
    recv_any,
    rows_ref,
    tiles_any,
    mass_ref,
    recv_ref,
    tiles_ref,
    kept_ref,
    left_ref,
    sums_ref,
    peak_ref,
    sems,
    weight_ref,
):
    load_recv = pltpu.make_async_copy(recv_any, recv_ref, sems.at[0])
    load_recv.start()
    load_tiles = pltpu.make_async_copy(tiles_any, tiles_ref, sems.at[1])
    load_tiles.start()
    tiles = tiles_ref.shape[0]
    groups, count = size_ref[0], size_ref[1]
    limit = jnp.minimum(groups, KEPT // G)
    row = lax.broadcasted_iota(jnp.int32, (8, BLK), 0)
    peak_ref[...] = jnp.full(peak_ref.shape, NEGATIVE, f32)
    sums_ref[...] = jnp.zeros(sums_ref.shape, f32)

    def find(g, carry):
        slot, tile, base = listed(list_ref, g, capacity)
        for k in range(G):
            at = pl.ds(tile[k], 1)
            peak_ref[at, :] = jnp.maximum(peak_ref[at, :], rows_ref[pl.ds(slot[k], 1), :])
        return carry

    lax.fori_loop(0, groups, find, 0)
    peak = jnp.max(peak_ref[...], axis=1, keepdims=True)
    peak_ref[...] = jnp.broadcast_to(COL_SHIFT - peak, peak_ref.shape)

    def prepare(g):
        slot, tile, base = listed(list_ref, g, capacity)
        for k in range(G):
            extra = rows_ref[pl.ds(slot[k], 1), :] + peak_ref[pl.ds(tile[k], 1), :]
            extra = jnp.broadcast_to(extra, (8, BLK))
            left_ref[k] = particle_rows(recv_ref, (base[k], capacity), extra, row)

    def powers(tile):
        raised = [product(left_ref[k], tiles_ref[tile[k]]) for k in range(G)]
        return [jnp.exp2(a) for a in raised]

    def first(keep, g, carry):
        slot, tile, base = listed(list_ref, g, capacity)
        power = powers(tile)
        prepare(jnp.minimum(g + 1, groups - 1))
        for k in range(G):
            if keep:
                kept_ref[g * G + k] = power[k]
            into = jnp.where(g * G + k < count, tile[k], tiles)
            sums_ref[into] += jnp.sum(power[k].reshape(BLK // 8, 8, TILE), axis=0)
        return carry

    load_recv.wait()
    prepare(0)
    load_tiles.wait()
    lax.fori_loop(0, limit, functools.partial(first, True), 0)
    lax.fori_loop(limit, groups, functools.partial(first, False), 0)
    total = jnp.sum(sums_ref[0:tiles], axis=1)
    weights(lanes_of(mass_ref) / total, weight_ref)

    def second_kept(g, carry):
        slot, tile, base = listed(list_ref, g, capacity)
        for k in range(G):
            store(slot[k], tile[k], kept_ref[g * G + k], weight_ref)
        return carry

    def second_rest(g, carry):
        slot, tile, base = listed(list_ref, g, capacity)
        prepare(g)
        power = powers(tile)
        for k in range(G):
            store(slot[k], tile[k], power[k], weight_ref)
        return carry

    lax.fori_loop(0, limit, second_kept, 0)
    lax.fori_loop(limit, groups, second_rest, 0)


def middle_kernel(
    capacity, list_ref, size_ref, recv_ref, rows_ref, tiles_ref, mass_ref, part_ref, *scratch
):
    def weights(value, weight_ref):
        weight_ref[...] = value

    def store(slot, tile, power, weight_ref):
        power = power * weight_ref[pl.ds(tile, 1), :]
        part_ref[pl.ds(slot, 1), :] = jnp.sum(fold_lanes(power).T, axis=0, keepdims=True)

    iterate(
        capacity,
        weights,
        store,
        list_ref,
        size_ref,
        recv_ref,
        rows_ref,
        tiles_ref,
        mass_ref,
        *scratch,
    )


def last_kernel(
    capacity,
    list_ref,
    size_ref,
    recv_ref,
    rows_ref,
    tiles_ref,
    mass_ref,
    sample_ref,
    part_ref,
    *scratch,
):
    *scratch, value_ref = scratch
    row = lax.broadcasted_iota(jnp.int32, (8, TILE), 0)

    def weights(value, weight_ref):
        value_ref[...] = value

        def body(t, carry):
            where = pl.ds(pl.multiple_of(t * TILE, TILE), TILE)
            place = jnp.ones((8, TILE), f32)
            for d in range(3):
                part = jnp.broadcast_to(sample_ref[d : d + 1, where], (8, TILE)) - 0.5
                place = jnp.where((row == d) | (row == d + 4), part, place)
            high, middle, low = split3(place * value_ref[pl.ds(t, 1), :])
            upper = jnp.where(row < 4, high, middle)
            lower = jnp.where(row < 4, low, 0.0)
            weight_ref[t] = jnp.concatenate([upper, lower], 0).astype(bf16)
            return carry

        lax.fori_loop(0, value_ref.shape[0], body, 0, unroll=4)

    def store(slot, tile, power, weight_ref):
        left = weight_ref[tile]
        high = power.astype(bf16)
        low = (power - high.astype(f32)).astype(bf16)
        dims = (((1,), (1,)), ((), ()))
        out = lax.dot_general(left, high, dims, preferred_element_type=f32)
        out = out + lax.dot_general(left, low, dims, preferred_element_type=f32)
        out = out[0:8] + out[8:16]
        part_ref[pl.ds(pl.multiple_of(slot * ROWS, ROWS), ROWS), :] = out[0:4] + out[4:8]

    iterate(
        capacity,
        weights,
        store,
        list_ref,
        size_ref,
        recv_ref,
        rows_ref,
        tiles_ref,
        mass_ref,
        *scratch,
    )


def local(
    positions,
    velocities,
    masses,
    samples,
    sample_mass,
    start_potential,
    route_owner,
    route_tile,
    live_count,
):
    devices = lax.axis_size("dev")
    blocks = route_owner.shape[0]
    tiles = start_potential.shape[0] // TILE
    capacity = 2 * blocks * K // devices
    slots = devices * capacity
    struct = jax.ShapeDtypeStruct

    def exchange(values):
        rows = values.shape[0] // devices
        got = lax.all_to_all(
            values.reshape(devices, rows, BLK), "dev", split_axis=0, concat_axis=0, tiled=True
        )
        return got.reshape(values.shape)

    send, slot = call(
        functools.partial(setup_kernel, capacity),
        (struct((slots * ROWS, BLK), f32), struct((blocks * K,), jnp.int32)),
        [SMEM, SMEM, SMEM, VMEM],
        (VMEM, SMEM),
        [pltpu.SMEM((devices,), jnp.int32)],
        10**6,
        (route_owner.T, route_tile.T, live_count, positions),
    )
    recv = exchange(send)
    split_tiles = call(
        sample_kernel,
        struct((tiles, DEPTH, TILE), bf16),
        [VMEM],
        VMEM,
        [],
        10**7,
        (samples,),
    )
    mass_rows = masses.reshape(blocks, BLK)
    sample_rows = sample_mass.reshape(tiles * CHUNKS, BLK)
    pot_rows = start_potential.reshape(tiles * CHUNKS, BLK)
    part, order, size = call(
        functools.partial(row_first_kernel, capacity),
        (struct((slots, BLK), f32), struct((slots + 2 * G,), jnp.int32), struct((2,), jnp.int32)),
        [VMEM, ANY, VMEM],
        (VMEM, SMEM, SMEM),
        [
            pltpu.VMEM((tiles, DEPTH, TILE), bf16),
            pltpu.VMEM((tiles, TILE), f32),
            pltpu.VMEM((tiles, BLK), f32),
            pltpu.VMEM((G, BLK, DEPTH), bf16),
            pltpu.VMEM((devices, BLK), jnp.int32),
            pltpu.SMEM((devices, BLK), jnp.int32),
            pltpu.SemaphoreType.DMA((2,)),
        ],
        10**9,
        (recv, split_tiles, pot_rows),
    )
    part = exchange(part)
    row_scratch = [pltpu.VMEM((K, blocks, BLK), f32)]
    row_out = (struct((slots, BLK), f32), struct((blocks, BLK), f32))
    send, row = call(
        home_first_kernel,
        row_out,
        [SMEM, SMEM, VMEM, VMEM],
        (VMEM, VMEM),
        row_scratch,
        10**6,
        (slot, live_count, part, mass_rows),
    )
    rows = exchange(send)
    scratch = [
        pltpu.VMEM((slots * ROWS, BLK), f32),
        pltpu.VMEM((tiles, DEPTH, TILE), bf16),
        pltpu.VMEM((min(KEPT, slots), BLK, TILE), f32),
        pltpu.VMEM((G, BLK, DEPTH), bf16),
        pltpu.VMEM((tiles + 1, 8, TILE), f32),
        pltpu.VMEM((tiles, BLK), f32),
        pltpu.SemaphoreType.DMA((2,)),
    ]
    values = pltpu.VMEM((tiles, TILE), f32)
    part = call(
        functools.partial(middle_kernel, capacity),
        struct((slots, BLK), f32),
        [SMEM, SMEM, ANY, VMEM, ANY, VMEM],
        VMEM,
        scratch + [values],
        10**9,
        (order, size, recv, rows, split_tiles, sample_rows),
    )
    part = exchange(part)
    send, row = call(
        home_next_kernel,
        row_out,
        [SMEM, SMEM, VMEM, VMEM, VMEM],
        (VMEM, VMEM),
        row_scratch,
        10**6,
        (slot, live_count, part, mass_rows, row),
    )
    rows = exchange(send)
    part = call(
        functools.partial(last_kernel, capacity),
        struct((slots * ROWS, BLK), f32),
        [SMEM, SMEM, ANY, VMEM, ANY, VMEM, VMEM],
        VMEM,
        scratch + [pltpu.VMEM((tiles, 16, TILE), bf16), values],
        10**9,
        (order, size, recv, rows, split_tiles, sample_rows, samples),
    )
    part = exchange(part)
    return call(
        home_last_kernel,
        (struct(positions.shape, f32), struct(positions.shape, f32)),
        [SMEM, SMEM, VMEM, VMEM, VMEM],
        (VMEM, VMEM),
        [],
        10**6,
        (slot, live_count, part, positions, velocities),
    )


def solution(mesh):
    placed = (
        P(None, "dev"),
        P(None, "dev"),
        P("dev"),
        P(None, "dev"),
        P("dev"),
        P("dev"),
        P("dev", None),
        P("dev", None),
        P("dev"),
    )
    return jax.shard_map(
        local,
        mesh=mesh,
        in_specs=placed,
        out_specs=(P(None, "dev"), P(None, "dev")),
        check_vma=False,
    )
```

```python
import functools
import jax
import jax.numpy as jnp
from jax import lax
from jax.experimental import pallas as pl
from jax.experimental.pallas import tpu as pltpu
from jax.sharding import PartitionSpec as P

BLK = 128
TILE = 512
K = 4
CHUNKS = TILE // BLK
EPSILON = 0.01
STIFFNESS = 150.0
TIMESTEP = 0.05
LOG2E = 1.4426950408889634
SCALE = LOG2E / EPSILON
NEGATIVE = -1e30
ROW_SHIFT = 115.0
COL_SHIFT = 110.0
G = 16
KEPT = 208
ROWS = 4
DEPTH = 32

f32 = jnp.float32
bf16 = jnp.bfloat16
VMEM = pl.BlockSpec(memory_space=pltpu.VMEM)
ANY = pl.BlockSpec(memory_space=pl.ANY)
SMEM = pl.BlockSpec(memory_space=pltpu.SMEM)


def call(kernel, out_shape, in_specs, out_specs, scratch, flops, args, limit=67_000_000):
    size = sum(a.size * a.dtype.itemsize for a in args)
    return pl.pallas_call(
        kernel,
        out_shape=out_shape,
        in_specs=in_specs,
        out_specs=out_specs,
        scratch_shapes=scratch,
        compiler_params=pltpu.CompilerParams(vmem_limit_bytes=limit),
        cost_estimate=pl.CostEstimate(flops=flops, bytes_accessed=size, transcendentals=0),
    )(*args)


def split3(value):
    high = value.astype(bf16).astype(f32)
    rest = value - high
    middle = rest.astype(bf16).astype(f32)
    return high, middle, rest - middle


def setup_kernel(capacity, owner_ref, tile_ref, live_ref, pos_ref, send_ref, slot_ref, count_ref):
    blocks = live_ref.shape[0]
    stride = capacity * ROWS

    def clear(i, carry):
        count_ref[i] = 0
        return carry

    lax.fori_loop(0, count_ref.shape[0], clear, 0)
    send_ref[...] = jnp.full(send_ref.shape, -1.0, f32)
    for b in range(blocks):
        rows = [pos_ref[d : d + 1, b * BLK : (b + 1) * BLK] for d in range(3)]
        for k in range(K):
            owner = owner_ref[k, b]
            rank = count_ref[owner]
            count_ref[owner] = rank + 1
            slot_ref[b * K + k] = owner * capacity + rank
            tile = jnp.where(k < live_ref[b], tile_ref[k, b], -1).astype(f32)
            base = owner * stride + rank
            for d in range(3):
                send_ref[pl.ds(base + d * capacity, 1), :] = rows[d]
            send_ref[pl.ds(base + 3 * capacity, 1), :] = jnp.full((1, BLK), tile, f32)


def home_gather(slot_ref, live_ref, recv_ref, parts_ref, filler):
    blocks = live_ref.shape[0]
    for b in range(blocks):
        live = live_ref[b]
        for k in range(K):
            row = recv_ref[pl.ds(slot_ref[b * K + k], 1), :]
            parts_ref[k, b : b + 1, :] = jnp.where(k < live, row, filler)


def home_scatter(slot_ref, rows_ref, send_ref):
    for b in range(rows_ref.shape[0]):
        row = rows_ref[b : b + 1, :]
        for k in range(K):
            send_ref[pl.ds(slot_ref[b * K + k], 1), :] = row


def home_first_kernel(slot_ref, live_ref, recv_ref, mass_ref, send_ref, row_ref, parts_ref):
    home_gather(slot_ref, live_ref, recv_ref, parts_ref, NEGATIVE)
    parts = parts_ref[...]
    top = jnp.max(parts, axis=0)
    total = jnp.sum(jnp.exp2(parts - top[None]), axis=0)
    row_ref[...] = jnp.log2(mass_ref[...]) - (top + jnp.log2(total))
    home_scatter(slot_ref, row_ref, send_ref)


def home_next_kernel(slot_ref, live_ref, recv_ref, mass_ref, old_ref, send_ref, row_ref, parts_ref):
    home_gather(slot_ref, live_ref, recv_ref, parts_ref, 0.0)
    total = jnp.sum(parts_ref[...], axis=0)
    row_ref[...] = old_ref[...] + jnp.log2(mass_ref[...]) - jnp.log2(total)
    home_scatter(slot_ref, row_ref, send_ref)


def home_last_kernel(slot_ref, live_ref, recv_ref, pos_ref, vel_ref, new_pos_ref, new_vel_ref):
    blocks = live_ref.shape[0]
    for b in range(blocks):
        live = live_ref[b]
        parts = jnp.zeros((ROWS, BLK), f32)
        for k in range(K):
            rows = recv_ref[pl.ds(slot_ref[b * K + k] * ROWS, ROWS), :]
            parts = parts + jnp.where(k < live, rows, 0.0)
        where = slice(b * BLK, (b + 1) * BLK)
        centre = parts[0:3] / parts[3:4] + 0.5
        here = pos_ref[:, where]
        velocity = vel_ref[:, where] + STIFFNESS * (centre - here)
        new_vel_ref[:, where] = velocity
        new_pos_ref[:, where] = here + TIMESTEP * velocity


def sample_kernel(sample_ref, tiles_ref):
    tiles = tiles_ref.shape[0]
    row = lax.broadcasted_iota(jnp.int32, (8, TILE), 0)

    def body(t, carry):
        where = pl.ds(pl.multiple_of(t * TILE, TILE), TILE)
        parts = [jnp.broadcast_to(sample_ref[d : d + 1, where], (8, TILE)) - 0.5 for d in range(3)]
        square = parts[0] * parts[0] + parts[1] * parts[1] + parts[2] * parts[2]
        value = (-0.5 * SCALE) * square
        for d in range(3):
            value = jnp.where((row == d) | (row == d + 5), parts[d], value)
        high, middle, low = split3(value)
        one = row == 3
        first = jnp.where(one, 1.0, jnp.where(row > 4, middle, high))
        second = jnp.where(one, 1.0, jnp.where(row > 4, low, middle))
        third = jnp.where(one, 1.0, jnp.where(row == 4, low, high))
        zero = jnp.zeros_like(first)
        tiles_ref[t] = jnp.concatenate([first, second, third, zero], 0).astype(bf16)
        return carry

    lax.fori_loop(0, tiles, body, 0, unroll=4)


def lanes_of(ref):
    tiles = ref.shape[0] // CHUNKS
    return jnp.concatenate([ref[pl.ds(c, tiles, stride=CHUNKS), :] for c in range(CHUNKS)], 1)


def particle_rows(recv_ref, place, extra, row):
    base, capacity = place
    parts = [
        (jnp.broadcast_to(recv_ref[pl.ds(base + d * capacity, 1), :], (8, BLK)) - 0.5)
        for d in range(3)
    ]
    square = parts[0] * parts[0] + parts[1] * parts[1] + parts[2] * parts[2]
    value = (-0.5 * SCALE) * square + extra
    for d in range(3):
        value = jnp.where((row == d) | (row == d + 5), SCALE * parts[d], value)
    high, middle, low = split3(value)
    one = row == 4
    first = jnp.where(one, 1.0, jnp.where(row > 4, middle, high))
    second = jnp.where(one, 1.0, jnp.where(row == 3, middle, high))
    third = jnp.where(one, 1.0, jnp.where(row < 3, middle, low))
    zero = jnp.zeros_like(first)
    return jnp.concatenate([first, second, third, zero], 0).astype(bf16).T


def fold_lanes(value):
    out = value[:, :BLK]
    for c in range(1, CHUNKS):
        out = out + value[:, c * BLK : (c + 1) * BLK]
    return out


def product(left, right):
    return jnp.dot(left, right, preferred_element_type=f32)


def unpack(list_ref, index, capacity):
    code = list_ref[index]
    slot = lax.shift_right_logical(code, 16)
    device = lax.div(slot, capacity)
    return slot, code & 0xFFFF, slot + device * (capacity * (ROWS - 1))


def listed(list_ref, g, capacity):
    slots = [unpack(list_ref, g * G + k, capacity) for k in range(G)]
    return [list(item) for item in zip(*slots)]


def row_first_kernel(
    capacity,
    recv_ref,
    tiles_any,
    pot_ref,
    part_ref,
    list_ref,
    size_ref,
    tiles_ref,
    beta_ref,
    top_ref,
    left_ref,
    asked_ref,
    tile_ref,
    sems,
):
    load = pltpu.make_async_copy(tiles_any, tiles_ref, sems.at[0])
    load.start()
    devices = asked_ref.shape[0]
    lane = lax.broadcasted_iota(jnp.int32, (devices, capacity, BLK), 2)
    rank = lax.broadcasted_iota(jnp.int32, (devices, capacity, BLK), 1)
    asked = recv_ref[...].reshape(devices, ROWS * capacity, BLK)[:, 3 * capacity :, :]
    asked_ref[...] = jnp.sum(jnp.where(lane == rank, asked, 0.0), axis=1).astype(jnp.int32)
    copy = pltpu.make_async_copy(asked_ref, tile_ref, sems.at[1])
    copy.start()

    pot = lanes_of(pot_ref) * SCALE
    top = jnp.max(pot, axis=1, keepdims=True)
    beta_ref[...] = pot - top
    top_ref[...] = jnp.broadcast_to(top - ROW_SHIFT, top_ref.shape)
    row = lax.broadcasted_iota(jnp.int32, (8, BLK), 0)
    copy.wait()

    def compact(device, count):
        for k in range(capacity):
            tile = tile_ref[device, k]
            list_ref[count] = ((device * capacity + k) << 16) + jnp.maximum(tile, 0)
            count = count + jnp.where(tile >= 0, 1, 0)
        return count

    count = lax.fori_loop(0, devices, compact, 0)
    groups = (count + G - 1) // G
    size_ref[0] = groups
    size_ref[1] = count
    for k in range(G):
        list_ref[count + k] = list_ref[0]

    def prepare(g):
        slot, tile, base = listed(list_ref, g, capacity)
        for k in range(G):
            left_ref[k] = particle_rows(recv_ref, (base[k], capacity), ROW_SHIFT, row)

    prepare(0)
    load.wait()

    def body(g, carry):
        slot, tile, base = listed(list_ref, g, capacity)
        raised = [product(left_ref[k], tiles_ref[tile[k]]) for k in range(G)]
        power = [jnp.exp2(a + beta_ref[pl.ds(t, 1), :]) for a, t in zip(raised, tile)]
        prepare(jnp.minimum(g + 1, groups - 1))
        total = [jnp.sum(fold_lanes(a).T, axis=0, keepdims=True) for a in power]
        for k in range(G):
            part_ref[pl.ds(slot[k], 1), :] = jnp.log2(total[k]) + top_ref[pl.ds(tile[k], 1), :]
        return carry

    lax.fori_loop(0, groups, body, 0)


def iterate(
    capacity,
    weights,
    store,
    list_ref,
    size_ref,
    recv_any,
    rows_ref,
    tiles_any,
    mass_ref,
    recv_ref,
    tiles_ref,
    kept_ref,
    left_ref,
    sums_ref,
    peak_ref,
    sems,
    weight_ref,
):
    load_recv = pltpu.make_async_copy(recv_any, recv_ref, sems.at[0])
    load_recv.start()
    load_tiles = pltpu.make_async_copy(tiles_any, tiles_ref, sems.at[1])
    load_tiles.start()
    tiles = tiles_ref.shape[0]
    groups, count = size_ref[0], size_ref[1]
    limit = jnp.minimum(groups, KEPT // G)
    row = lax.broadcasted_iota(jnp.int32, (8, BLK), 0)
    peak_ref[...] = jnp.full(peak_ref.shape, NEGATIVE, f32)
    sums_ref[...] = jnp.zeros(sums_ref.shape, f32)

    def find(g, carry):
        slot, tile, base = listed(list_ref, g, capacity)
        for k in range(G):
            at = pl.ds(tile[k], 1)
            peak_ref[at, :] = jnp.maximum(peak_ref[at, :], rows_ref[pl.ds(slot[k], 1), :])
        return carry

    lax.fori_loop(0, groups, find, 0)
    peak = jnp.max(peak_ref[...], axis=1, keepdims=True)
    peak_ref[...] = jnp.broadcast_to(COL_SHIFT - peak, peak_ref.shape)

    def prepare(g):
        slot, tile, base = listed(list_ref, g, capacity)
        for k in range(G):
            extra = rows_ref[pl.ds(slot[k], 1), :] + peak_ref[pl.ds(tile[k], 1), :]
            extra = jnp.broadcast_to(extra, (8, BLK))
            left_ref[k] = particle_rows(recv_ref, (base[k], capacity), extra, row)

    def powers(tile):
        raised = [product(left_ref[k], tiles_ref[tile[k]]) for k in range(G)]
        return [jnp.exp2(a) for a in raised]

    def first(keep, g, carry):
        slot, tile, base = listed(list_ref, g, capacity)
        power = powers(tile)
        prepare(jnp.minimum(g + 1, groups - 1))
        for k in range(G):
            if keep:
                kept_ref[g * G + k] = power[k]
            into = jnp.where(g * G + k < count, tile[k], tiles)
            sums_ref[into] += jnp.sum(power[k].reshape(BLK // 8, 8, TILE), axis=0)
        return carry

    load_recv.wait()
    prepare(0)
    load_tiles.wait()
    lax.fori_loop(0, limit, functools.partial(first, True), 0)
    lax.fori_loop(limit, groups, functools.partial(first, False), 0)
    total = jnp.sum(sums_ref[0:tiles], axis=1)
    weights(lanes_of(mass_ref) / total, weight_ref)

    def second_kept(g, carry):
        slot, tile, base = listed(list_ref, g, capacity)
        for k in range(G):
            store(slot[k], tile[k], kept_ref[g * G + k], weight_ref)
        return carry

    def second_rest(g, carry):
        slot, tile, base = listed(list_ref, g, capacity)
        prepare(g)
        power = powers(tile)
        for k in range(G):
            store(slot[k], tile[k], power[k], weight_ref)
        return carry

    lax.fori_loop(0, limit, second_kept, 0)
    lax.fori_loop(limit, groups, second_rest, 0)


def middle_kernel(
    capacity, list_ref, size_ref, recv_ref, rows_ref, tiles_ref, mass_ref, part_ref, *scratch
):
    def weights(value, weight_ref):
        weight_ref[...] = value

    def store(slot, tile, power, weight_ref):
        power = power * weight_ref[pl.ds(tile, 1), :]
        part_ref[pl.ds(slot, 1), :] = jnp.sum(fold_lanes(power).T, axis=0, keepdims=True)

    iterate(
        capacity,
        weights,
        store,
        list_ref,
        size_ref,
        recv_ref,
        rows_ref,
        tiles_ref,
        mass_ref,
        *scratch,
    )


def last_kernel(
    capacity,
    list_ref,
    size_ref,
    recv_ref,
    rows_ref,
    tiles_ref,
    mass_ref,
    sample_ref,
    part_ref,
    *scratch,
):
    *scratch, value_ref = scratch
    row = lax.broadcasted_iota(jnp.int32, (8, TILE), 0)

    def weights(value, weight_ref):
        value_ref[...] = value

        def body(t, carry):
            where = pl.ds(pl.multiple_of(t * TILE, TILE), TILE)
            place = jnp.ones((8, TILE), f32)
            for d in range(3):
                part = jnp.broadcast_to(sample_ref[d : d + 1, where], (8, TILE)) - 0.5
                place = jnp.where((row == d) | (row == d + 4), part, place)
            high, middle, low = split3(place * value_ref[pl.ds(t, 1), :])
            upper = jnp.where(row < 4, high, middle)
            lower = jnp.where(row < 4, low, 0.0)
            weight_ref[t] = jnp.concatenate([upper, lower], 0).astype(bf16)
            return carry

        lax.fori_loop(0, value_ref.shape[0], body, 0, unroll=4)

    def store(slot, tile, power, weight_ref):
        left = weight_ref[tile]
        high = power.astype(bf16)
        low = (power - high.astype(f32)).astype(bf16)
        dims = (((1,), (1,)), ((), ()))
        out = lax.dot_general(left, high, dims, preferred_element_type=f32)
        out = out + lax.dot_general(left, low, dims, preferred_element_type=f32)
        out = out[0:8] + out[8:16]
        part_ref[pl.ds(pl.multiple_of(slot * ROWS, ROWS), ROWS), :] = out[0:4] + out[4:8]

    iterate(
        capacity,
        weights,
        store,
        list_ref,
        size_ref,
        recv_ref,
        rows_ref,
        tiles_ref,
        mass_ref,
        *scratch,
    )


def local(
    positions,
    velocities,
    masses,
    samples,
    sample_mass,
    start_potential,
    route_owner,
    route_tile,
    live_count,
):
    devices = lax.axis_size("dev")
    blocks = route_owner.shape[0]
    tiles = start_potential.shape[0] // TILE
    capacity = 2 * blocks * K // devices
    slots = devices * capacity
    struct = jax.ShapeDtypeStruct

    def exchange(values):
        rows = values.shape[0] // devices
        got = lax.all_to_all(
            values.reshape(devices, rows, BLK), "dev", split_axis=0, concat_axis=0, tiled=True
        )
        return got.reshape(values.shape)

    send, slot = call(
        functools.partial(setup_kernel, capacity),
        (struct((slots * ROWS, BLK), f32), struct((blocks * K,), jnp.int32)),
        [SMEM, SMEM, SMEM, VMEM],
        (VMEM, SMEM),
        [pltpu.SMEM((devices,), jnp.int32)],
        10**6,
        (route_owner.T, route_tile.T, live_count, positions),
        4 * 2**20,
    )
    recv = exchange(send)
    split_tiles = call(
        sample_kernel,
        struct((tiles, DEPTH, TILE), bf16),
        [VMEM],
        VMEM,
        [],
        10**7,
        (samples,),
        8 * 2**20,
    )
    mass_rows = masses.reshape(blocks, BLK)
    sample_rows = sample_mass.reshape(tiles * CHUNKS, BLK)
    pot_rows = start_potential.reshape(tiles * CHUNKS, BLK)
    part, order, size = call(
        functools.partial(row_first_kernel, capacity),
        (struct((slots, BLK), f32), struct((slots + 2 * G,), jnp.int32), struct((2,), jnp.int32)),
        [VMEM, ANY, VMEM],
        (VMEM, SMEM, SMEM),
        [
            pltpu.VMEM((tiles, DEPTH, TILE), bf16),
            pltpu.VMEM((tiles, TILE), f32),
            pltpu.VMEM((tiles, BLK), f32),
            pltpu.VMEM((G, BLK, DEPTH), bf16),
            pltpu.VMEM((devices, BLK), jnp.int32),
            pltpu.SMEM((devices, BLK), jnp.int32),
            pltpu.SemaphoreType.DMA((2,)),
        ],
        10**9,
        (recv, split_tiles, pot_rows),
        16 * 2**20,
    )
    part = exchange(part)
    row_scratch = [pltpu.VMEM((K, blocks, BLK), f32)]
    row_out = (struct((slots, BLK), f32), struct((blocks, BLK), f32))
    send, row = call(
        home_first_kernel,
        row_out,
        [SMEM, SMEM, VMEM, VMEM],
        (VMEM, VMEM),
        row_scratch,
        10**6,
        (slot, live_count, part, mass_rows),
        4 * 2**20,
    )
    rows = exchange(send)
    scratch = [
        pltpu.VMEM((slots * ROWS, BLK), f32),
        pltpu.VMEM((tiles, DEPTH, TILE), bf16),
        pltpu.VMEM((min(KEPT, slots), BLK, TILE), f32),
        pltpu.VMEM((G, BLK, DEPTH), bf16),
        pltpu.VMEM((tiles + 1, 8, TILE), f32),
        pltpu.VMEM((tiles, BLK), f32),
        pltpu.SemaphoreType.DMA((2,)),
    ]
    values = pltpu.VMEM((tiles, TILE), f32)
    part = call(
        functools.partial(middle_kernel, capacity),
        struct((slots, BLK), f32),
        [SMEM, SMEM, ANY, VMEM, ANY, VMEM],
        VMEM,
        scratch + [values],
        10**9,
        (order, size, recv, rows, split_tiles, sample_rows),
    )
    part = exchange(part)
    send, row = call(
        home_next_kernel,
        row_out,
        [SMEM, SMEM, VMEM, VMEM, VMEM],
        (VMEM, VMEM),
        row_scratch,
        10**6,
        (slot, live_count, part, mass_rows, row),
        4 * 2**20,
    )
    rows = exchange(send)
    part = call(
        functools.partial(last_kernel, capacity),
        struct((slots * ROWS, BLK), f32),
        [SMEM, SMEM, ANY, VMEM, ANY, VMEM, VMEM],
        VMEM,
        scratch + [pltpu.VMEM((tiles, 16, TILE), bf16), values],
        10**9,
        (order, size, recv, rows, split_tiles, sample_rows, samples),
    )
    part = exchange(part)
    return call(
        home_last_kernel,
        (struct(positions.shape, f32), struct(positions.shape, f32)),
        [SMEM, SMEM, VMEM, VMEM, VMEM],
        (VMEM, VMEM),
        [],
        10**6,
        (slot, live_count, part, positions, velocities),
        4 * 2**20,
    )


def solution(mesh):
    placed = (
        P(None, "dev"),
        P(None, "dev"),
        P("dev"),
        P(None, "dev"),
        P("dev"),
        P("dev"),
        P("dev", None),
        P("dev", None),
        P("dev"),
    )
    return jax.shard_map(
        local,
        mesh=mesh,
        in_specs=placed,
        out_specs=(P(None, "dev"), P(None, "dev")),
        check_vma=False,
    )
```

```python
import functools
import jax
import jax.numpy as jnp
from jax import lax
from jax.experimental import pallas as pl
from jax.experimental.pallas import tpu as pltpu
from jax.sharding import PartitionSpec as P

BLK = 128
TILE = 512
K = 4
CHUNKS = TILE // BLK
EPSILON = 0.01
STIFFNESS = 150.0
TIMESTEP = 0.05
LOG2E = 1.4426950408889634
SCALE = LOG2E / EPSILON
NEGATIVE = -1e30
ROW_SHIFT = 115.0
COL_SHIFT = 110.0
G = 16
KEPT_MIDDLE = 176
KEPT_LAST = 160
ROWS = 4
DEPTH = 32

LARGE = 50 * 2**20
f32 = jnp.float32
bf16 = jnp.bfloat16
VMEM = pl.BlockSpec(memory_space=pltpu.VMEM)
HBM = pl.BlockSpec(memory_space=pltpu.HBM)
SMEM = pl.BlockSpec(memory_space=pltpu.SMEM)


def call(kernel, out_shape, in_specs, out_specs, scratch, flops, args, limit=LARGE):
    size = sum(a.size * a.dtype.itemsize for a in args)
    return pl.pallas_call(
        kernel,
        out_shape=out_shape,
        in_specs=in_specs,
        out_specs=out_specs,
        scratch_shapes=scratch,
        compiler_params=pltpu.CompilerParams(vmem_limit_bytes=limit),
        cost_estimate=pl.CostEstimate(flops=flops, bytes_accessed=size, transcendentals=0),
    )(*args)


def split3(value):
    high = value.astype(bf16).astype(f32)
    rest = value - high
    middle = rest.astype(bf16).astype(f32)
    return high, middle, rest - middle


def setup_kernel(capacity, owner_ref, tile_ref, live_ref, pos_ref, send_ref, slot_ref, count_ref):
    blocks = live_ref.shape[0]
    stride = capacity * ROWS

    def clear(i, carry):
        count_ref[i] = 0
        return carry

    lax.fori_loop(0, count_ref.shape[0], clear, 0)
    send_ref[...] = jnp.full(send_ref.shape, -1.0, f32)
    for b in range(blocks):
        rows = [pos_ref[d : d + 1, b * BLK : (b + 1) * BLK] for d in range(3)]
        for k in range(K):
            owner = owner_ref[k, b]
            rank = count_ref[owner]
            count_ref[owner] = rank + 1
            slot_ref[b * K + k] = owner * capacity + rank
            tile = jnp.where(k < live_ref[b], tile_ref[k, b], -1).astype(f32)
            base = owner * stride + rank
            for d in range(3):
                send_ref[pl.ds(base + d * capacity, 1), :] = rows[d]
            send_ref[pl.ds(base + 3 * capacity, 1), :] = jnp.full((1, BLK), tile, f32)


def home_gather(slot_ref, live_ref, recv_ref, parts_ref, filler):
    blocks = live_ref.shape[0]
    for b in range(blocks):
        live = live_ref[b]
        for k in range(K):
            row = recv_ref[pl.ds(slot_ref[b * K + k], 1), :]
            parts_ref[k, b : b + 1, :] = jnp.where(k < live, row, filler)


def home_scatter(slot_ref, rows_ref, send_ref):
    for b in range(rows_ref.shape[0]):
        row = rows_ref[b : b + 1, :]
        for k in range(K):
            send_ref[pl.ds(slot_ref[b * K + k], 1), :] = row


def home_first_kernel(slot_ref, live_ref, recv_ref, mass_ref, send_ref, row_ref, parts_ref):
    home_gather(slot_ref, live_ref, recv_ref, parts_ref, NEGATIVE)
    parts = parts_ref[...]
    top = jnp.max(parts, axis=0)
    total = jnp.sum(jnp.exp2(parts - top[None]), axis=0)
    row_ref[...] = jnp.log2(mass_ref[...]) - (top + jnp.log2(total))
    home_scatter(slot_ref, row_ref, send_ref)


def home_next_kernel(slot_ref, live_ref, recv_ref, mass_ref, old_ref, send_ref, row_ref, parts_ref):
    home_gather(slot_ref, live_ref, recv_ref, parts_ref, 0.0)
    total = jnp.sum(parts_ref[...], axis=0)
    row_ref[...] = old_ref[...] + jnp.log2(mass_ref[...]) - jnp.log2(total)
    home_scatter(slot_ref, row_ref, send_ref)


def home_last_kernel(
    slot_ref, live_ref, recv_ref, pos_hbm, vel_hbm, new_pos_ref, new_vel_ref, pos_ref, vel_ref, sems
):
    loads = [
        pltpu.make_async_copy(pos_hbm, pos_ref, sems.at[0]),
        pltpu.make_async_copy(vel_hbm, vel_ref, sems.at[1]),
    ]
    for load in loads:
        load.start()
    for load in loads:
        load.wait()
    blocks = live_ref.shape[0]
    for b in range(blocks):
        live = live_ref[b]
        parts = jnp.zeros((ROWS, BLK), f32)
        for k in range(K):
            rows = recv_ref[pl.ds(slot_ref[b * K + k] * ROWS, ROWS), :]
            parts = parts + jnp.where(k < live, rows, 0.0)
        where = slice(b * BLK, (b + 1) * BLK)
        centre = parts[0:3] / parts[3:4] + 0.5
        here = pos_ref[:, where]
        velocity = vel_ref[:, where] + STIFFNESS * (centre - here)
        new_vel_ref[:, where] = velocity
        new_pos_ref[:, where] = here + TIMESTEP * velocity


def sample_kernel(sample_ref, tiles_ref):
    tiles = tiles_ref.shape[0]
    row = lax.broadcasted_iota(jnp.int32, (8, TILE), 0)

    def body(t, carry):
        where = pl.ds(pl.multiple_of(t * TILE, TILE), TILE)
        parts = [jnp.broadcast_to(sample_ref[d : d + 1, where], (8, TILE)) - 0.5 for d in range(3)]
        square = parts[0] * parts[0] + parts[1] * parts[1] + parts[2] * parts[2]
        value = (-0.5 * SCALE) * square
        for d in range(3):
            value = jnp.where((row == d) | (row == d + 5), parts[d], value)
        high, middle, low = split3(value)
        one = row == 3
        first = jnp.where(one, 1.0, jnp.where(row > 4, middle, high))
        second = jnp.where(one, 1.0, jnp.where(row > 4, low, middle))
        third = jnp.where(one, 1.0, jnp.where(row == 4, low, high))
        zero = jnp.zeros_like(first)
        tiles_ref[t] = jnp.concatenate([first, second, third, zero], 0).astype(bf16)
        return carry

    lax.fori_loop(0, tiles, body, 0, unroll=4)


def lanes_of(ref):
    tiles = ref.shape[0] // CHUNKS
    return jnp.concatenate([ref[pl.ds(c, tiles, stride=CHUNKS), :] for c in range(CHUNKS)], 1)


def particle_rows(recv_ref, place, extra, row):
    base, capacity = place
    parts = [
        (jnp.broadcast_to(recv_ref[pl.ds(base + d * capacity, 1), :], (8, BLK)) - 0.5)
        for d in range(3)
    ]
    square = parts[0] * parts[0] + parts[1] * parts[1] + parts[2] * parts[2]
    value = (-0.5 * SCALE) * square + extra
    for d in range(3):
        value = jnp.where((row == d) | (row == d + 5), SCALE * parts[d], value)
    high, middle, low = split3(value)
    one = row == 4
    first = jnp.where(one, 1.0, jnp.where(row > 4, middle, high))
    second = jnp.where(one, 1.0, jnp.where(row == 3, middle, high))
    third = jnp.where(one, 1.0, jnp.where(row < 3, middle, low))
    zero = jnp.zeros_like(first)
    return jnp.concatenate([first, second, third, zero], 0).astype(bf16).T


def fold_lanes(value):
    out = value[:, :BLK]
    for c in range(1, CHUNKS):
        out = out + value[:, c * BLK : (c + 1) * BLK]
    return out


def product(left, right):
    return jnp.dot(left, right, preferred_element_type=f32)


def unpack(list_ref, index, capacity):
    code = list_ref[index]
    slot = lax.shift_right_logical(code, 16)
    device = lax.div(slot, capacity)
    return slot, code & 0xFFFF, slot + device * (capacity * (ROWS - 1))


def listed(list_ref, g, capacity):
    slots = [unpack(list_ref, g * G + k, capacity) for k in range(G)]
    return [list(item) for item in zip(*slots)]


def row_first_kernel(
    capacity,
    recv_ref,
    tiles_ref,
    pot_ref,
    part_ref,
    list_ref,
    size_ref,
    beta_ref,
    top_ref,
    left_ref,
    asked_ref,
    tile_ref,
    sem,
):
    devices = asked_ref.shape[0]
    lane = lax.broadcasted_iota(jnp.int32, (devices, capacity, BLK), 2)
    rank = lax.broadcasted_iota(jnp.int32, (devices, capacity, BLK), 1)
    asked = recv_ref[...].reshape(devices, ROWS * capacity, BLK)[:, 3 * capacity :, :]
    asked_ref[...] = jnp.sum(jnp.where(lane == rank, asked, 0.0), axis=1).astype(jnp.int32)
    copy = pltpu.make_async_copy(asked_ref, tile_ref, sem)
    copy.start()

    pot = lanes_of(pot_ref) * SCALE
    top = jnp.max(pot, axis=1, keepdims=True)
    beta_ref[...] = pot - top
    top_ref[...] = jnp.broadcast_to(top - ROW_SHIFT, top_ref.shape)
    row = lax.broadcasted_iota(jnp.int32, (8, BLK), 0)
    copy.wait()

    def compact(device, count):
        for k in range(capacity):
            tile = tile_ref[device, k]
            list_ref[count] = ((device * capacity + k) << 16) + jnp.maximum(tile, 0)
            count = count + jnp.where(tile >= 0, 1, 0)
        return count

    count = lax.fori_loop(0, devices, compact, 0)
    groups = (count + G - 1) // G
    size_ref[0] = groups
    size_ref[1] = count
    for k in range(G):
        list_ref[count + k] = list_ref[0]

    def prepare(g):
        slot, tile, base = listed(list_ref, g, capacity)
        for k in range(G):
            left_ref[k] = particle_rows(recv_ref, (base[k], capacity), ROW_SHIFT, row)

    prepare(0)

    def body(g, carry):
        slot, tile, base = listed(list_ref, g, capacity)
        raised = [product(left_ref[k], tiles_ref[tile[k]]) for k in range(G)]
        power = [jnp.exp2(a + beta_ref[pl.ds(t, 1), :]) for a, t in zip(raised, tile)]
        prepare(jnp.minimum(g + 1, groups - 1))
        total = [jnp.sum(fold_lanes(a).T, axis=0, keepdims=True) for a in power]
        for k in range(G):
            part_ref[pl.ds(slot[k], 1), :] = jnp.log2(total[k]) + top_ref[pl.ds(tile[k], 1), :]
        return carry

    lax.fori_loop(0, groups, body, 0)


def iterate(
    capacity,
    weights,
    store,
    list_ref,
    size_ref,
    recv_ref,
    rows_ref,
    tiles_ref,
    mass_ref,
    kept_ref,
    left_ref,
    sums_ref,
    peak_ref,
    weight_ref,
):
    tiles = tiles_ref.shape[0]
    groups, count = size_ref[0], size_ref[1]
    limit = jnp.minimum(groups, kept_ref.shape[0] // G)
    row = lax.broadcasted_iota(jnp.int32, (8, BLK), 0)
    peak_ref[...] = jnp.full(peak_ref.shape, NEGATIVE, f32)
    sums_ref[...] = jnp.zeros(sums_ref.shape, f32)

    def find(g, carry):
        slot, tile, base = listed(list_ref, g, capacity)
        for k in range(G):
            at = pl.ds(tile[k], 1)
            peak_ref[at, :] = jnp.maximum(peak_ref[at, :], rows_ref[pl.ds(slot[k], 1), :])
        return carry

    lax.fori_loop(0, groups, find, 0)
    peak = jnp.max(peak_ref[...], axis=1, keepdims=True)
    peak_ref[...] = jnp.broadcast_to(COL_SHIFT - peak, peak_ref.shape)

    def prepare(g):
        slot, tile, base = listed(list_ref, g, capacity)
        for k in range(G):
            extra = rows_ref[pl.ds(slot[k], 1), :] + peak_ref[pl.ds(tile[k], 1), :]
            extra = jnp.broadcast_to(extra, (8, BLK))
            left_ref[k] = particle_rows(recv_ref, (base[k], capacity), extra, row)

    def powers(tile):
        raised = [product(left_ref[k], tiles_ref[tile[k]]) for k in range(G)]
        return [jnp.exp2(a) for a in raised]

    def first(keep, g, carry):
        slot, tile, base = listed(list_ref, g, capacity)
        power = powers(tile)
        prepare(jnp.minimum(g + 1, groups - 1))
        for k in range(G):
            if keep:
                kept_ref[g * G + k] = power[k]
            into = jnp.where(g * G + k < count, tile[k], tiles)
            sums_ref[into] += jnp.sum(power[k].reshape(BLK // 8, 8, TILE), axis=0)
        return carry

    prepare(0)
    lax.fori_loop(0, limit, functools.partial(first, True), 0)
    lax.fori_loop(limit, groups, functools.partial(first, False), 0)
    total = jnp.sum(sums_ref[0:tiles], axis=1)
    weights(lanes_of(mass_ref) / total, weight_ref)

    def second_kept(g, carry):
        slot, tile, base = listed(list_ref, g, capacity)
        for k in range(G):
            store(slot[k], tile[k], kept_ref[g * G + k], weight_ref)
        return carry

    def second_rest(g, carry):
        slot, tile, base = listed(list_ref, g, capacity)
        prepare(g)
        for k in range(G):
            power = jnp.exp2(product(left_ref[k], tiles_ref[tile[k]]))
            store(slot[k], tile[k], power, weight_ref)
        return carry

    lax.fori_loop(0, limit, second_kept, 0)
    lax.fori_loop(limit, groups, second_rest, 0)


def middle_kernel(
    capacity, list_ref, size_ref, recv_ref, rows_ref, tiles_ref, mass_ref, part_ref, *scratch
):
    def weights(value, weight_ref):
        weight_ref[...] = value

    def store(slot, tile, power, weight_ref):
        power = power * weight_ref[pl.ds(tile, 1), :]
        part_ref[pl.ds(slot, 1), :] = jnp.sum(fold_lanes(power).T, axis=0, keepdims=True)

    iterate(
        capacity,
        weights,
        store,
        list_ref,
        size_ref,
        recv_ref,
        rows_ref,
        tiles_ref,
        mass_ref,
        *scratch,
    )


def last_kernel(
    capacity,
    list_ref,
    size_ref,
    recv_ref,
    rows_ref,
    tiles_ref,
    mass_ref,
    sample_ref,
    part_ref,
    *scratch,
):
    *scratch, value_ref = scratch
    row = lax.broadcasted_iota(jnp.int32, (8, TILE), 0)

    def weights(value, weight_ref):
        value_ref[...] = value

        def body(t, carry):
            where = pl.ds(pl.multiple_of(t * TILE, TILE), TILE)
            place = jnp.ones((8, TILE), f32)
            for d in range(3):
                part = jnp.broadcast_to(sample_ref[d : d + 1, where], (8, TILE)) - 0.5
                place = jnp.where((row == d) | (row == d + 4), part, place)
            high, middle, low = split3(place * value_ref[pl.ds(t, 1), :])
            upper = jnp.where(row < 4, high, middle)
            lower = jnp.where(row < 4, low, 0.0)
            weight_ref[t] = jnp.concatenate([upper, lower], 0).astype(bf16)
            return carry

        lax.fori_loop(0, value_ref.shape[0], body, 0, unroll=4)

    def store(slot, tile, power, weight_ref):
        left = weight_ref[tile]
        high = power.astype(bf16)
        low = (power - high.astype(f32)).astype(bf16)
        dims = (((1,), (1,)), ((), ()))
        out = lax.dot_general(left, high, dims, preferred_element_type=f32)
        out = out + lax.dot_general(left, low, dims, preferred_element_type=f32)
        out = out[0:8] + out[8:16]
        part_ref[pl.ds(pl.multiple_of(slot * ROWS, ROWS), ROWS), :] = out[0:4] + out[4:8]

    iterate(
        capacity,
        weights,
        store,
        list_ref,
        size_ref,
        recv_ref,
        rows_ref,
        tiles_ref,
        mass_ref,
        *scratch,
    )


def local(
    positions,
    velocities,
    masses,
    samples,
    sample_mass,
    start_potential,
    route_owner,
    route_tile,
    live_count,
):
    devices = lax.axis_size("dev")
    blocks = route_owner.shape[0]
    tiles = start_potential.shape[0] // TILE
    capacity = 2 * blocks * K // devices
    slots = devices * capacity
    struct = jax.ShapeDtypeStruct

    def exchange(values):
        rows = values.shape[0] // devices
        got = lax.all_to_all(
            values.reshape(devices, rows, BLK), "dev", split_axis=0, concat_axis=0, tiled=True
        )
        return got.reshape(values.shape)

    send, slot = call(
        functools.partial(setup_kernel, capacity),
        (struct((slots * ROWS, BLK), f32), struct((blocks * K,), jnp.int32)),
        [SMEM, SMEM, SMEM, VMEM],
        (VMEM, SMEM),
        [pltpu.SMEM((devices,), jnp.int32)],
        10**6,
        (route_owner.T, route_tile.T, live_count, positions),
        67_000_000,
    )
    recv = exchange(send)
    split_tiles = call(
        sample_kernel,
        struct((tiles, DEPTH, TILE), bf16),
        [VMEM],
        VMEM,
        [],
        10**7,
        (samples,),
        8 * 2**20,
    )
    mass_rows = masses.reshape(blocks, BLK)
    sample_rows = sample_mass.reshape(tiles * CHUNKS, BLK)
    pot_rows = start_potential.reshape(tiles * CHUNKS, BLK)
    part, order, size = call(
        functools.partial(row_first_kernel, capacity),
        (struct((slots, BLK), f32), struct((slots + 2 * G,), jnp.int32), struct((2,), jnp.int32)),
        [VMEM, VMEM, VMEM],
        (VMEM, SMEM, SMEM),
        [
            pltpu.VMEM((tiles, TILE), f32),
            pltpu.VMEM((tiles, BLK), f32),
            pltpu.VMEM((G, BLK, DEPTH), bf16),
            pltpu.VMEM((devices, BLK), jnp.int32),
            pltpu.SMEM((devices, BLK), jnp.int32),
            pltpu.SemaphoreType.DMA,
        ],
        10**9,
        (recv, split_tiles, pot_rows),
        16 * 2**20,
    )
    part = exchange(part)
    row_scratch = [pltpu.VMEM((K, blocks, BLK), f32)]
    row_out = (struct((slots, BLK), f32), struct((blocks, BLK), f32))
    send, row = call(
        home_first_kernel,
        row_out,
        [SMEM, SMEM, VMEM, VMEM],
        (VMEM, VMEM),
        row_scratch,
        10**6,
        (slot, live_count, part, mass_rows),
        4 * 2**20,
    )
    rows = exchange(send)
    keep = [pltpu.VMEM((min(k, slots), BLK, TILE), f32) for k in (KEPT_MIDDLE, KEPT_LAST)]
    scratch = [
        pltpu.VMEM((G, BLK, DEPTH), bf16),
        pltpu.VMEM((tiles + 1, 8, TILE), f32),
        pltpu.VMEM((tiles, BLK), f32),
    ]
    values = pltpu.VMEM((tiles, TILE), f32)
    part = call(
        functools.partial(middle_kernel, capacity),
        struct((slots, BLK), f32),
        [SMEM, SMEM] + [VMEM] * 4,
        VMEM,
        keep[:1] + scratch + [values],
        10**9,
        (order, size, recv, rows, split_tiles, sample_rows),
    )
    part = exchange(part)
    send, row = call(
        home_next_kernel,
        row_out,
        [SMEM, SMEM, VMEM, VMEM, VMEM],
        (VMEM, VMEM),
        row_scratch,
        10**6,
        (slot, live_count, part, mass_rows, row),
        4 * 2**20,
    )
    rows = exchange(send)
    part = call(
        functools.partial(last_kernel, capacity),
        struct((slots * ROWS, BLK), f32),
        [SMEM, SMEM] + [VMEM] * 5,
        VMEM,
        keep[1:] + scratch + [pltpu.VMEM((tiles, 16, TILE), bf16), values],
        10**9,
        (order, size, recv, rows, split_tiles, sample_rows, samples),
    )
    part = exchange(part)
    return call(
        home_last_kernel,
        (struct(positions.shape, f32), struct(positions.shape, f32)),
        [SMEM, SMEM, VMEM, HBM, HBM],
        (VMEM, VMEM),
        [
            pltpu.VMEM(positions.shape, f32),
            pltpu.VMEM(positions.shape, f32),
            pltpu.SemaphoreType.DMA((2,)),
        ],
        10**6,
        (slot, live_count, part, positions, velocities),
        4 * 2**20,
    )


def solution(mesh):
    placed = (
        P(None, "dev"),
        P(None, "dev"),
        P("dev"),
        P(None, "dev"),
        P("dev"),
        P("dev"),
        P("dev", None),
        P("dev", None),
        P("dev"),
    )
    return jax.shard_map(
        local,
        mesh=mesh,
        in_specs=placed,
        out_specs=(P(None, "dev"), P(None, "dev")),
        check_vma=False,
    )
```

```python
import functools
import jax
import jax.numpy as jnp
from jax import lax
from jax.experimental import pallas as pl
from jax.experimental.pallas import tpu as pltpu
from jax.sharding import PartitionSpec as P

BLK = 128
TILE = 512
K = 4
CHUNKS = TILE // BLK
EPSILON = 0.01
STIFFNESS = 150.0
TIMESTEP = 0.05
LOG2E = 1.4426950408889634
SCALE = LOG2E / EPSILON
NEGATIVE = -1e30
ROW_SHIFT = 115.0
COL_SHIFT = 110.0
G = 16
KEPT = 144
HALVES = 2
ROWS = 4
DEPTH = 32

LARGE = 44 * 2**20
f32 = jnp.float32
bf16 = jnp.bfloat16
VMEM = pl.BlockSpec(memory_space=pltpu.VMEM)
HBM = pl.BlockSpec(memory_space=pltpu.HBM)
SMEM = pl.BlockSpec(memory_space=pltpu.SMEM)


def call(kernel, out_shape, in_specs, out_specs, scratch, flops, args, limit=LARGE):
    size = sum(a.size * a.dtype.itemsize for a in args)
    return pl.pallas_call(
        kernel,
        out_shape=out_shape,
        in_specs=in_specs,
        out_specs=out_specs,
        scratch_shapes=scratch,
        compiler_params=pltpu.CompilerParams(vmem_limit_bytes=limit),
        cost_estimate=pl.CostEstimate(flops=flops, bytes_accessed=size, transcendentals=0),
    )(*args)


def split3(value):
    high = value.astype(bf16).astype(f32)
    rest = value - high
    middle = rest.astype(bf16).astype(f32)
    return high, middle, rest - middle


def setup_kernel(capacity, owner_ref, tile_ref, live_ref, pos_ref, send_ref, slot_ref, count_ref):
    blocks = live_ref.shape[0]
    stride = capacity * ROWS

    def clear(i, carry):
        count_ref[i] = 0
        return carry

    lax.fori_loop(0, count_ref.shape[0], clear, 0)
    send_ref[...] = jnp.full(send_ref.shape, -1.0, f32)
    for b in range(blocks):
        rows = [pos_ref[d : d + 1, b * BLK : (b + 1) * BLK] for d in range(3)]
        for k in range(K):
            owner = owner_ref[k, b]
            rank = count_ref[owner]
            count_ref[owner] = rank + 1
            slot_ref[b * K + k] = owner * capacity + rank
            tile = jnp.where(k < live_ref[b], tile_ref[k, b], -1).astype(f32)
            base = owner * stride + rank
            for d in range(3):
                send_ref[pl.ds(base + d * capacity, 1), :] = rows[d]
            send_ref[pl.ds(base + 3 * capacity, 1), :] = jnp.full((1, BLK), tile, f32)


def home_gather(slot_ref, live_ref, recv_ref, parts_ref, filler):
    blocks = live_ref.shape[0]
    for b in range(blocks):
        live = live_ref[b]
        for k in range(K):
            row = recv_ref[pl.ds(slot_ref[b * K + k], 1), :]
            parts_ref[k, b : b + 1, :] = jnp.where(k < live, row, filler)


def home_scatter(slot_ref, rows_ref, send_ref):
    for b in range(rows_ref.shape[0]):
        row = rows_ref[b : b + 1, :]
        for k in range(K):
            send_ref[pl.ds(slot_ref[b * K + k], 1), :] = row


def home_first_kernel(slot_ref, live_ref, recv_ref, mass_ref, send_ref, row_ref, parts_ref):
    home_gather(slot_ref, live_ref, recv_ref, parts_ref, NEGATIVE)
    parts = parts_ref[...]
    top = jnp.max(parts, axis=0)
    total = jnp.sum(jnp.exp2(parts - top[None]), axis=0)
    row_ref[...] = jnp.log2(mass_ref[...]) - (top + jnp.log2(total))
    home_scatter(slot_ref, row_ref, send_ref)


def home_next_kernel(slot_ref, live_ref, recv_ref, mass_ref, old_ref, send_ref, row_ref, parts_ref):
    home_gather(slot_ref, live_ref, recv_ref, parts_ref, 0.0)
    total = jnp.sum(parts_ref[...], axis=0)
    row_ref[...] = old_ref[...] + jnp.log2(mass_ref[...]) - jnp.log2(total)
    home_scatter(slot_ref, row_ref, send_ref)


def home_last_kernel(
    slot_ref, live_ref, recv_ref, pos_hbm, vel_hbm, new_pos_ref, new_vel_ref, pos_ref, vel_ref, sems
):
    loads = [
        pltpu.make_async_copy(pos_hbm, pos_ref, sems.at[0]),
        pltpu.make_async_copy(vel_hbm, vel_ref, sems.at[1]),
    ]
    for load in loads:
        load.start()
    for load in loads:
        load.wait()
    blocks = live_ref.shape[0]
    for b in range(blocks):
        live = live_ref[b]
        parts = jnp.zeros((ROWS, BLK), f32)
        for k in range(K):
            rows = recv_ref[pl.ds(slot_ref[b * K + k] * ROWS, ROWS), :]
            parts = parts + jnp.where(k < live, rows, 0.0)
        where = slice(b * BLK, (b + 1) * BLK)
        centre = parts[0:3] / parts[3:4] + 0.5
        here = pos_ref[:, where]
        velocity = vel_ref[:, where] + STIFFNESS * (centre - here)
        new_vel_ref[:, where] = velocity
        new_pos_ref[:, where] = here + TIMESTEP * velocity


def sample_kernel(sample_ref, tiles_ref):
    tiles = tiles_ref.shape[0]
    row = lax.broadcasted_iota(jnp.int32, (8, TILE), 0)

    def body(t, carry):
        where = pl.ds(pl.multiple_of(t * TILE, TILE), TILE)
        parts = [jnp.broadcast_to(sample_ref[d : d + 1, where], (8, TILE)) - 0.5 for d in range(3)]
        square = parts[0] * parts[0] + parts[1] * parts[1] + parts[2] * parts[2]
        value = (-0.5 * SCALE) * square
        for d in range(3):
            value = jnp.where((row == d) | (row == d + 5), parts[d], value)
        high, middle, low = split3(value)
        one = row == 3
        first = jnp.where(one, 1.0, jnp.where(row > 4, middle, high))
        second = jnp.where(one, 1.0, jnp.where(row > 4, low, middle))
        third = jnp.where(one, 1.0, jnp.where(row == 4, low, high))
        zero = jnp.zeros_like(first)
        tiles_ref[t] = jnp.concatenate([first, second, third, zero], 0).astype(bf16)
        return carry

    lax.fori_loop(0, tiles, body, 0, unroll=4)


def lanes_of(ref):
    tiles = ref.shape[0] // CHUNKS
    return jnp.concatenate([ref[pl.ds(c, tiles, stride=CHUNKS), :] for c in range(CHUNKS)], 1)


def particle_rows(recv_ref, place, extra, row):
    base, capacity = place
    parts = [
        (jnp.broadcast_to(recv_ref[pl.ds(base + d * capacity, 1), :], (8, BLK)) - 0.5)
        for d in range(3)
    ]
    square = parts[0] * parts[0] + parts[1] * parts[1] + parts[2] * parts[2]
    value = (-0.5 * SCALE) * square + extra
    for d in range(3):
        value = jnp.where((row == d) | (row == d + 5), SCALE * parts[d], value)
    high, middle, low = split3(value)
    one = row == 4
    first = jnp.where(one, 1.0, jnp.where(row > 4, middle, high))
    second = jnp.where(one, 1.0, jnp.where(row == 3, middle, high))
    third = jnp.where(one, 1.0, jnp.where(row < 3, middle, low))
    zero = jnp.zeros_like(first)
    return jnp.concatenate([first, second, third, zero], 0).astype(bf16).T


def fold_lanes(value):
    out = value[:, :BLK]
    for c in range(1, CHUNKS):
        out = out + value[:, c * BLK : (c + 1) * BLK]
    return out


def product(left, right):
    return jnp.dot(left, right, preferred_element_type=f32)


def unpack(list_ref, index, capacity):
    code = list_ref[index]
    slot = lax.shift_right_logical(code, 16)
    device = lax.div(slot, capacity)
    return slot, code & 0xFFFF, slot + device * (capacity * (ROWS - 1))


def part_start(h, slots):
    return h * (slots + 2 * G)


def listed(list_ref, start, capacity):
    slots = [unpack(list_ref, start + k, capacity) for k in range(G)]
    return [list(item) for item in zip(*slots)]


def row_first_kernel(
    capacity,
    recv_ref,
    tiles_ref,
    pot_ref,
    part_ref,
    list_ref,
    size_ref,
    beta_ref,
    top_ref,
    left_ref,
    asked_ref,
    tile_ref,
    sem,
):
    devices = asked_ref.shape[0]
    lane = lax.broadcasted_iota(jnp.int32, (devices, capacity, BLK), 2)
    rank = lax.broadcasted_iota(jnp.int32, (devices, capacity, BLK), 1)
    asked = recv_ref[...].reshape(devices, ROWS * capacity, BLK)[:, 3 * capacity :, :]
    asked_ref[...] = jnp.sum(jnp.where(lane == rank, asked, 0.0), axis=1).astype(jnp.int32)
    copy = pltpu.make_async_copy(asked_ref, tile_ref, sem)
    copy.start()

    pot = lanes_of(pot_ref) * SCALE
    top = jnp.max(pot, axis=1, keepdims=True)
    beta_ref[...] = pot - top
    top_ref[...] = jnp.broadcast_to(top - ROW_SHIFT, top_ref.shape)
    row = lax.broadcasted_iota(jnp.int32, (8, BLK), 0)
    copy.wait()

    slots = devices * capacity
    half = tiles_ref.shape[0] // HALVES

    def compact(device, counts):
        for k in range(capacity):
            tile = tile_ref[device, k]
            upper = tile >= half
            place = jnp.where(upper, part_start(1, slots) + counts[1], counts[0])
            list_ref[place] = ((device * capacity + k) << 16) + jnp.maximum(tile, 0)
            low = jnp.where((tile >= 0) & (tile < half), 1, 0)
            counts = (counts[0] + low, counts[1] + jnp.where(upper, 1, 0))
        return counts

    zero = jnp.int32(0)
    counts = lax.fori_loop(0, devices, compact, (zero, zero))
    for h in range(HALVES):
        size_ref[h] = counts[h]
        start = part_start(h, slots)
        list_ref[start + counts[h]] = 0
        for k in range(G):
            list_ref[start + counts[h] + k] = list_ref[start]

    def run(h):
        start = part_start(h, slots)
        groups = (counts[h] + G - 1) // G

        def prepare(g):
            slot, tile, base = listed(list_ref, start + g * G, capacity)
            for k in range(G):
                left_ref[k] = particle_rows(recv_ref, (base[k], capacity), ROW_SHIFT, row)

        prepare(0)

        def body(g, carry):
            slot, tile, base = listed(list_ref, start + g * G, capacity)
            raised = [product(left_ref[k], tiles_ref[tile[k]]) for k in range(G)]
            power = [jnp.exp2(a + beta_ref[pl.ds(t, 1), :]) for a, t in zip(raised, tile)]
            prepare(jnp.minimum(g + 1, groups - 1))
            total = [jnp.sum(fold_lanes(a).T, axis=0, keepdims=True) for a in power]
            for k in range(G):
                part_ref[pl.ds(slot[k], 1), :] = (
                    jnp.log2(total[k]) + top_ref[pl.ds(tile[k], 1), :]
                )
            return carry

        lax.fori_loop(0, groups, body, 0)

    for h in range(HALVES):
        run(h)


def iterate(
    capacity,
    weights,
    store,
    list_ref,
    size_ref,
    recv_ref,
    rows_ref,
    tiles_ref,
    mass_ref,
    kept_ref,
    left_ref,
    sums_ref,
    peak_ref,
    weight_ref,
):
    tiles = tiles_ref.shape[0]
    slots = rows_ref.shape[0]
    half = tiles // HALVES
    row = lax.broadcasted_iota(jnp.int32, (8, BLK), 0)
    peak_ref[...] = jnp.full(peak_ref.shape, NEGATIVE, f32)
    sums_ref[...] = jnp.zeros(sums_ref.shape, f32)
    mass = lanes_of(mass_ref)

    for h in range(HALVES):

        def find(g, carry, start=part_start(h, slots)):
            slot, tile, base = listed(list_ref, start + g * G, capacity)
            for k in range(G):
                at = pl.ds(tile[k], 1)
                peak_ref[at, :] = jnp.maximum(peak_ref[at, :], rows_ref[pl.ds(slot[k], 1), :])
            return carry

        lax.fori_loop(0, (size_ref[h] + G - 1) // G, find, 0)
    peak = jnp.max(peak_ref[...], axis=1, keepdims=True)
    peak_ref[...] = jnp.broadcast_to(COL_SHIFT - peak, peak_ref.shape)

    def part(h):
        start = part_start(h, slots)
        count = size_ref[h]
        groups = (count + G - 1) // G
        limit = jnp.minimum(groups, kept_ref.shape[0] // G)

        def prepare(g):
            slot, tile, base = listed(list_ref, start + g * G, capacity)
            for k in range(G):
                extra = rows_ref[pl.ds(slot[k], 1), :] + peak_ref[pl.ds(tile[k], 1), :]
                extra = jnp.broadcast_to(extra, (8, BLK))
                left_ref[k] = particle_rows(recv_ref, (base[k], capacity), extra, row)

        def power(k, tile):
            return jnp.exp2(product(left_ref[k], tiles_ref[tile[k]]))

        def first(keep, g, carry):
            slot, tile, base = listed(list_ref, start + g * G, capacity)
            raised = [power(k, tile) for k in range(G)]
            prepare(jnp.minimum(g + 1, groups - 1))
            for k in range(G):
                if keep:
                    kept_ref[g * G + k] = raised[k]
                into = jnp.where(g * G + k < count, tile[k], tiles)
                sums_ref[into] += jnp.sum(raised[k].reshape(BLK // 8, 8, TILE), axis=0)
            return carry

        prepare(0)
        lax.fori_loop(0, limit, functools.partial(first, True), 0)
        lax.fori_loop(limit, groups, functools.partial(first, False), 0)
        here = slice(h * half, (h + 1) * half)
        total = jnp.sum(sums_ref[here], axis=1)
        weights(h * half, mass[here] / total, weight_ref)

        def second_kept(g, carry):
            slot, tile, base = listed(list_ref, start + g * G, capacity)
            for k in range(G):
                store(slot[k], tile[k], kept_ref[g * G + k], weight_ref)
            return carry

        def second_rest(g, carry):
            slot, tile, base = listed(list_ref, start + g * G, capacity)
            prepare(g)
            for k in range(G):
                store(slot[k], tile[k], power(k, tile), weight_ref)
            return carry

        lax.fori_loop(0, limit, second_kept, 0)
        lax.fori_loop(limit, groups, second_rest, 0)

    for h in range(HALVES):
        part(h)


def middle_kernel(
    capacity, list_ref, size_ref, recv_ref, rows_ref, tiles_ref, mass_ref, part_ref, *scratch
):
    def weights(start, value, weight_ref):
        weight_ref[start : start + value.shape[0], :] = value

    def store(slot, tile, power, weight_ref):
        power = power * weight_ref[pl.ds(tile, 1), :]
        part_ref[pl.ds(slot, 1), :] = jnp.sum(fold_lanes(power).T, axis=0, keepdims=True)

    iterate(
        capacity,
        weights,
        store,
        list_ref,
        size_ref,
        recv_ref,
        rows_ref,
        tiles_ref,
        mass_ref,
        *scratch,
    )


def last_kernel(
    capacity,
    list_ref,
    size_ref,
    recv_ref,
    rows_ref,
    tiles_ref,
    mass_ref,
    sample_ref,
    part_ref,
    *scratch,
):
    *scratch, value_ref = scratch
    row = lax.broadcasted_iota(jnp.int32, (8, TILE), 0)

    def weights(start, value, weight_ref):
        value_ref[start : start + value.shape[0], :] = value

        def body(t, carry):
            where = pl.ds(pl.multiple_of(t * TILE, TILE), TILE)
            place = jnp.ones((8, TILE), f32)
            for d in range(3):
                part = jnp.broadcast_to(sample_ref[d : d + 1, where], (8, TILE)) - 0.5
                place = jnp.where((row == d) | (row == d + 4), part, place)
            high, middle, low = split3(place * value_ref[pl.ds(t, 1), :])
            upper = jnp.where(row < 4, high, middle)
            lower = jnp.where(row < 4, low, 0.0)
            weight_ref[t] = jnp.concatenate([upper, lower], 0).astype(bf16)
            return carry

        lax.fori_loop(start, start + value.shape[0], body, 0, unroll=4)

    def store(slot, tile, power, weight_ref):
        left = weight_ref[tile]
        high = power.astype(bf16)
        low = (power - high.astype(f32)).astype(bf16)
        dims = (((1,), (1,)), ((), ()))
        out = lax.dot_general(left, high, dims, preferred_element_type=f32)
        out = out + lax.dot_general(left, low, dims, preferred_element_type=f32)
        out = out[0:8] + out[8:16]
        part_ref[pl.ds(pl.multiple_of(slot * ROWS, ROWS), ROWS), :] = out[0:4] + out[4:8]

    iterate(
        capacity,
        weights,
        store,
        list_ref,
        size_ref,
        recv_ref,
        rows_ref,
        tiles_ref,
        mass_ref,
        *scratch,
    )


def local(
    positions,
    velocities,
    masses,
    samples,
    sample_mass,
    start_potential,
    route_owner,
    route_tile,
    live_count,
):
    devices = lax.axis_size("dev")
    blocks = route_owner.shape[0]
    tiles = start_potential.shape[0] // TILE
    capacity = 2 * blocks * K // devices
    slots = devices * capacity
    struct = jax.ShapeDtypeStruct

    def exchange(values):
        rows = values.shape[0] // devices
        got = lax.all_to_all(
            values.reshape(devices, rows, BLK), "dev", split_axis=0, concat_axis=0, tiled=True
        )
        return got.reshape(values.shape)

    send, slot = call(
        functools.partial(setup_kernel, capacity),
        (struct((slots * ROWS, BLK), f32), struct((blocks * K,), jnp.int32)),
        [SMEM, SMEM, SMEM, VMEM],
        (VMEM, SMEM),
        [pltpu.SMEM((devices,), jnp.int32)],
        10**6,
        (route_owner.T, route_tile.T, live_count, positions),
        67_000_000,
    )
    recv = exchange(send)
    split_tiles = call(
        sample_kernel,
        struct((tiles, DEPTH, TILE), bf16),
        [VMEM],
        VMEM,
        [],
        10**7,
        (samples,),
        8 * 2**20,
    )
    mass_rows = masses.reshape(blocks, BLK)
    sample_rows = sample_mass.reshape(tiles * CHUNKS, BLK)
    pot_rows = start_potential.reshape(tiles * CHUNKS, BLK)
    part, order, size = call(
        functools.partial(row_first_kernel, capacity),
        (struct((slots, BLK), f32), struct((HALVES * (slots + 2 * G),), jnp.int32), struct((HALVES,), jnp.int32)),
        [VMEM, VMEM, VMEM],
        (VMEM, SMEM, SMEM),
        [
            pltpu.VMEM((tiles, TILE), f32),
            pltpu.VMEM((tiles, BLK), f32),
            pltpu.VMEM((G, BLK, DEPTH), bf16),
            pltpu.VMEM((devices, BLK), jnp.int32),
            pltpu.SMEM((devices, BLK), jnp.int32),
            pltpu.SemaphoreType.DMA,
        ],
        10**9,
        (recv, split_tiles, pot_rows),
        16 * 2**20,
    )
    part = exchange(part)
    row_scratch = [pltpu.VMEM((K, blocks, BLK), f32)]
    row_out = (struct((slots, BLK), f32), struct((blocks, BLK), f32))
    send, row = call(
        home_first_kernel,
        row_out,
        [SMEM, SMEM, VMEM, VMEM],
        (VMEM, VMEM),
        row_scratch,
        10**6,
        (slot, live_count, part, mass_rows),
        4 * 2**20,
    )
    rows = exchange(send)
    scratch = [
        pltpu.VMEM((min(KEPT, slots), BLK, TILE), f32),
        pltpu.VMEM((G, BLK, DEPTH), bf16),
        pltpu.VMEM((tiles + 1, 8, TILE), f32),
        pltpu.VMEM((tiles, BLK), f32),
    ]
    values = pltpu.VMEM((tiles, TILE), f32)
    part = call(
        functools.partial(middle_kernel, capacity),
        struct((slots, BLK), f32),
        [SMEM, SMEM] + [VMEM] * 4,
        VMEM,
        scratch + [values],
        10**9,
        (order, size, recv, rows, split_tiles, sample_rows),
    )
    part = exchange(part)
    send, row = call(
        home_next_kernel,
        row_out,
        [SMEM, SMEM, VMEM, VMEM, VMEM],
        (VMEM, VMEM),
        row_scratch,
        10**6,
        (slot, live_count, part, mass_rows, row),
        4 * 2**20,
    )
    rows = exchange(send)
    part = call(
        functools.partial(last_kernel, capacity),
        struct((slots * ROWS, BLK), f32),
        [SMEM, SMEM] + [VMEM] * 5,
        VMEM,
        scratch + [pltpu.VMEM((tiles, 16, TILE), bf16), values],
        10**9,
        (order, size, recv, rows, split_tiles, sample_rows, samples),
    )
    part = exchange(part)
    return call(
        home_last_kernel,
        (struct(positions.shape, f32), struct(positions.shape, f32)),
        [SMEM, SMEM, VMEM, HBM, HBM],
        (VMEM, VMEM),
        [
            pltpu.VMEM(positions.shape, f32),
            pltpu.VMEM(positions.shape, f32),
            pltpu.SemaphoreType.DMA((2,)),
        ],
        10**6,
        (slot, live_count, part, positions, velocities),
        4 * 2**20,
    )


def solution(mesh):
    placed = (
        P(None, "dev"),
        P(None, "dev"),
        P("dev"),
        P(None, "dev"),
        P("dev"),
        P("dev"),
        P("dev", None),
        P("dev", None),
        P("dev"),
    )
    return jax.shard_map(
        local,
        mesh=mesh,
        in_specs=placed,
        out_specs=(P(None, "dev"), P(None, "dev")),
        check_vma=False,
    )
```

```python
import functools
import jax
import jax.numpy as jnp
from jax import lax
from jax.experimental import pallas as pl
from jax.experimental.pallas import tpu as pltpu
from jax.sharding import PartitionSpec as P

BLK = 128
TILE = 512
K = 4
CHUNKS = TILE // BLK
EPSILON = 0.01
STIFFNESS = 150.0
TIMESTEP = 0.05
LOG2E = 1.4426950408889634
SCALE = LOG2E / EPSILON
NEGATIVE = -1e30
ROW_SHIFT = 115.0
COL_SHIFT = 110.0
G = 16
KEPT = 144
HALVES = 2
ROWS = 4
DEPTH = 32

LARGE = 44 * 2**20
f32 = jnp.float32
bf16 = jnp.bfloat16
VMEM = pl.BlockSpec(memory_space=pltpu.VMEM)
SMEM = pl.BlockSpec(memory_space=pltpu.SMEM)


def call(kernel, out_shape, in_specs, out_specs, scratch, flops, args, limit=LARGE):
    size = sum(a.size * a.dtype.itemsize for a in args)
    return pl.pallas_call(
        kernel,
        out_shape=out_shape,
        in_specs=in_specs,
        out_specs=out_specs,
        scratch_shapes=scratch,
        compiler_params=pltpu.CompilerParams(vmem_limit_bytes=limit),
        cost_estimate=pl.CostEstimate(flops=flops, bytes_accessed=size, transcendentals=0),
    )(*args)


def split3(value):
    high = value.astype(bf16).astype(f32)
    rest = value - high
    middle = rest.astype(bf16).astype(f32)
    return high, middle, rest - middle


def setup_kernel(capacity, owner_ref, tile_ref, live_ref, pos_ref, send_ref, slot_ref, count_ref):
    blocks = live_ref.shape[0]
    stride = capacity * ROWS

    def clear(i, carry):
        count_ref[i] = 0
        return carry

    lax.fori_loop(0, count_ref.shape[0], clear, 0)
    send_ref[...] = jnp.full(send_ref.shape, -1.0, f32)
    for b in range(blocks):
        rows = [pos_ref[d : d + 1, b * BLK : (b + 1) * BLK] for d in range(3)]
        for k in range(K):
            owner = owner_ref[k, b]
            rank = count_ref[owner]
            count_ref[owner] = rank + 1
            slot_ref[b * K + k] = owner * capacity + rank
            tile = jnp.where(k < live_ref[b], tile_ref[k, b], -1).astype(f32)
            base = owner * stride + rank
            for d in range(3):
                send_ref[pl.ds(base + d * capacity, 1), :] = rows[d]
            send_ref[pl.ds(base + 3 * capacity, 1), :] = jnp.full((1, BLK), tile, f32)


def home_gather(slot_ref, live_ref, recv_ref, parts_ref, filler):
    blocks = live_ref.shape[0]
    for b in range(blocks):
        live = live_ref[b]
        for k in range(K):
            row = recv_ref[pl.ds(slot_ref[b * K + k], 1), :]
            parts_ref[k, b : b + 1, :] = jnp.where(k < live, row, filler)


def home_scatter(slot_ref, rows_ref, send_ref):
    for b in range(rows_ref.shape[0]):
        row = rows_ref[b : b + 1, :]
        for k in range(K):
            send_ref[pl.ds(slot_ref[b * K + k], 1), :] = row


def home_first_kernel(slot_ref, live_ref, recv_ref, mass_ref, send_ref, row_ref, parts_ref):
    home_gather(slot_ref, live_ref, recv_ref, parts_ref, NEGATIVE)
    parts = parts_ref[...]
    top = jnp.max(parts, axis=0)
    total = jnp.sum(jnp.exp2(parts - top[None]), axis=0)
    row_ref[...] = jnp.log2(mass_ref[...]) - (top + jnp.log2(total))
    home_scatter(slot_ref, row_ref, send_ref)


def home_next_kernel(slot_ref, live_ref, recv_ref, mass_ref, old_ref, send_ref, row_ref, parts_ref):
    home_gather(slot_ref, live_ref, recv_ref, parts_ref, 0.0)
    total = jnp.sum(parts_ref[...], axis=0)
    row_ref[...] = old_ref[...] + jnp.log2(mass_ref[...]) - jnp.log2(total)
    home_scatter(slot_ref, row_ref, send_ref)


def home_last_kernel(slot_ref, live_ref, recv_ref, pos_ref, vel_ref, new_pos_ref, new_vel_ref):
    blocks = live_ref.shape[0]
    for b in range(blocks):
        live = live_ref[b]
        parts = jnp.zeros((ROWS, BLK), f32)
        for k in range(K):
            rows = recv_ref[pl.ds(slot_ref[b * K + k] * ROWS, ROWS), :]
            parts = parts + jnp.where(k < live, rows, 0.0)
        where = slice(b * BLK, (b + 1) * BLK)
        centre = parts[0:3] / parts[3:4] + 0.5
        here = pos_ref[:, where]
        velocity = vel_ref[:, where] + STIFFNESS * (centre - here)
        new_vel_ref[:, where] = velocity
        new_pos_ref[:, where] = here + TIMESTEP * velocity


def sample_kernel(sample_ref, tiles_ref):
    tiles = tiles_ref.shape[0]
    row = lax.broadcasted_iota(jnp.int32, (8, TILE), 0)

    def body(t, carry):
        where = pl.ds(pl.multiple_of(t * TILE, TILE), TILE)
        parts = [jnp.broadcast_to(sample_ref[d : d + 1, where], (8, TILE)) - 0.5 for d in range(3)]
        square = parts[0] * parts[0] + parts[1] * parts[1] + parts[2] * parts[2]
        value = (-0.5 * SCALE) * square
        for d in range(3):
            value = jnp.where((row == d) | (row == d + 5), parts[d], value)
        high, middle, low = split3(value)
        one = row == 3
        first = jnp.where(one, 1.0, jnp.where(row > 4, middle, high))
        second = jnp.where(one, 1.0, jnp.where(row > 4, low, middle))
        third = jnp.where(one, 1.0, jnp.where(row == 4, low, high))
        zero = jnp.zeros_like(first)
        tiles_ref[t] = jnp.concatenate([first, second, third, zero], 0).astype(bf16)
        return carry

    lax.fori_loop(0, tiles, body, 0, unroll=4)


def lanes_of(ref):
    tiles = ref.shape[0] // CHUNKS
    return jnp.concatenate([ref[pl.ds(c, tiles, stride=CHUNKS), :] for c in range(CHUNKS)], 1)


def particle_rows(recv_ref, place, extra, row):
    base, capacity = place
    parts = [
        (jnp.broadcast_to(recv_ref[pl.ds(base + d * capacity, 1), :], (8, BLK)) - 0.5)
        for d in range(3)
    ]
    square = parts[0] * parts[0] + parts[1] * parts[1] + parts[2] * parts[2]
    value = (-0.5 * SCALE) * square + extra
    for d in range(3):
        value = jnp.where((row == d) | (row == d + 5), SCALE * parts[d], value)
    high, middle, low = split3(value)
    one = row == 4
    first = jnp.where(one, 1.0, jnp.where(row > 4, middle, high))
    second = jnp.where(one, 1.0, jnp.where(row == 3, middle, high))
    third = jnp.where(one, 1.0, jnp.where(row < 3, middle, low))
    zero = jnp.zeros_like(first)
    return jnp.concatenate([first, second, third, zero], 0).astype(bf16).T


def fold_lanes(value):
    out = value[:, :BLK]
    for c in range(1, CHUNKS):
        out = out + value[:, c * BLK : (c + 1) * BLK]
    return out


def product(left, right):
    return jnp.dot(left, right, preferred_element_type=f32)


def unpack(list_ref, index, capacity):
    code = list_ref[index]
    slot = lax.shift_right_logical(code, 16)
    device = lax.div(slot, capacity)
    return slot, code & 0xFFFF, slot + device * (capacity * (ROWS - 1))


def part_start(h, slots):
    return h * (slots + 2 * G)


def listed(list_ref, start, capacity):
    slots = [unpack(list_ref, start + k, capacity) for k in range(G)]
    return [list(item) for item in zip(*slots)]


def row_first_kernel(
    capacity,
    recv_ref,
    tiles_ref,
    pot_ref,
    part_ref,
    list_ref,
    size_ref,
    beta_ref,
    top_ref,
    left_ref,
    asked_ref,
    tile_ref,
    all_ref,
    sem,
):
    devices = asked_ref.shape[0]
    lane = lax.broadcasted_iota(jnp.int32, (devices, capacity, BLK), 2)
    rank = lax.broadcasted_iota(jnp.int32, (devices, capacity, BLK), 1)
    asked = recv_ref[...].reshape(devices, ROWS * capacity, BLK)[:, 3 * capacity :, :]
    asked_ref[...] = jnp.sum(jnp.where(lane == rank, asked, 0.0), axis=1).astype(jnp.int32)
    copy = pltpu.make_async_copy(asked_ref, tile_ref, sem)
    copy.start()

    pot = lanes_of(pot_ref) * SCALE
    top = jnp.max(pot, axis=1, keepdims=True)
    beta_ref[...] = pot - top
    top_ref[...] = jnp.broadcast_to(top - ROW_SHIFT, top_ref.shape)
    row = lax.broadcasted_iota(jnp.int32, (8, BLK), 0)
    copy.wait()

    slots = devices * capacity
    half = tiles_ref.shape[0] // HALVES

    def compact(device, counts):
        for k in range(capacity):
            tile = tile_ref[device, k]
            upper = tile >= half
            code = ((device * capacity + k) << 16) + jnp.maximum(tile, 0)
            all_ref[counts[0] + counts[1]] = code
            place = jnp.where(upper, part_start(1, slots) + counts[1], counts[0])
            list_ref[place] = code
            low = jnp.where((tile >= 0) & (tile < half), 1, 0)
            counts = (counts[0] + low, counts[1] + jnp.where(upper, 1, 0))
        return counts

    zero = jnp.int32(0)
    counts = lax.fori_loop(0, devices, compact, (zero, zero))
    for h in range(HALVES):
        size_ref[h] = counts[h]
        start = part_start(h, slots)
        list_ref[start + counts[h]] = 0
        for k in range(G):
            list_ref[start + counts[h] + k] = list_ref[start]

    count = counts[0] + counts[1]
    groups = (count + G - 1) // G
    all_ref[count] = 0
    for k in range(G):
        all_ref[count + k] = all_ref[0]

    def prepare(g):
        slot, tile, base = listed(all_ref, g * G, capacity)
        for k in range(G):
            left_ref[k] = particle_rows(recv_ref, (base[k], capacity), ROW_SHIFT, row)

    prepare(0)

    def body(g, carry):
        slot, tile, base = listed(all_ref, g * G, capacity)
        raised = [product(left_ref[k], tiles_ref[tile[k]]) for k in range(G)]
        power = [jnp.exp2(a + beta_ref[pl.ds(t, 1), :]) for a, t in zip(raised, tile)]
        prepare(jnp.minimum(g + 1, groups - 1))
        total = [jnp.sum(fold_lanes(a).T, axis=0, keepdims=True) for a in power]
        for k in range(G):
            part_ref[pl.ds(slot[k], 1), :] = jnp.log2(total[k]) + top_ref[pl.ds(tile[k], 1), :]
        return carry

    lax.fori_loop(0, groups, body, 0)


def iterate(
    capacity,
    weights,
    store,
    list_ref,
    size_ref,
    recv_ref,
    rows_ref,
    tiles_ref,
    mass_ref,
    kept_ref,
    left_ref,
    sums_ref,
    peak_ref,
    weight_ref,
):
    tiles = tiles_ref.shape[0]
    slots = rows_ref.shape[0]
    half = tiles // HALVES
    row = lax.broadcasted_iota(jnp.int32, (8, BLK), 0)
    peak_ref[...] = jnp.full(peak_ref.shape, NEGATIVE, f32)
    sums_ref[...] = jnp.zeros(sums_ref.shape, f32)
    mass = lanes_of(mass_ref)

    for h in range(HALVES):

        def find(g, carry, start=part_start(h, slots)):
            slot, tile, base = listed(list_ref, start + g * G, capacity)
            for k in range(G):
                at = pl.ds(tile[k], 1)
                peak_ref[at, :] = jnp.maximum(peak_ref[at, :], rows_ref[pl.ds(slot[k], 1), :])
            return carry

        lax.fori_loop(0, (size_ref[h] + G - 1) // G, find, 0)
    peak = jnp.max(peak_ref[...], axis=1, keepdims=True)
    peak_ref[...] = jnp.broadcast_to(COL_SHIFT - peak, peak_ref.shape)

    def part(h):
        start = part_start(h, slots)
        count = size_ref[h]
        groups = (count + G - 1) // G
        limit = jnp.minimum(groups, kept_ref.shape[0] // G)

        def prepare(g):
            slot, tile, base = listed(list_ref, start + g * G, capacity)
            for k in range(G):
                extra = rows_ref[pl.ds(slot[k], 1), :] + peak_ref[pl.ds(tile[k], 1), :]
                extra = jnp.broadcast_to(extra, (8, BLK))
                left_ref[k] = particle_rows(recv_ref, (base[k], capacity), extra, row)

        def power(k, tile):
            return jnp.exp2(product(left_ref[k], tiles_ref[tile[k]]))

        def first(keep, g, carry):
            slot, tile, base = listed(list_ref, start + g * G, capacity)
            raised = [power(k, tile) for k in range(G)]
            prepare(jnp.minimum(g + 1, groups - 1))
            for k in range(G):
                if keep:
                    kept_ref[g * G + k] = raised[k]
                into = jnp.where(g * G + k < count, tile[k], tiles)
                sums_ref[into] += jnp.sum(raised[k].reshape(BLK // 8, 8, TILE), axis=0)
            return carry

        prepare(0)
        lax.fori_loop(0, limit, functools.partial(first, True), 0)
        lax.fori_loop(limit, groups, functools.partial(first, False), 0)
        here = slice(h * half, (h + 1) * half)
        total = jnp.sum(sums_ref[here], axis=1)
        weights(h * half, mass[here] / total, weight_ref)

        def second_kept(g, carry):
            slot, tile, base = listed(list_ref, start + g * G, capacity)
            for k in range(G):
                store(slot[k], tile[k], kept_ref[g * G + k], weight_ref)
            return carry

        def second_rest(g, carry):
            slot, tile, base = listed(list_ref, start + g * G, capacity)
            prepare(g)
            for k in range(G):
                store(slot[k], tile[k], power(k, tile), weight_ref)
            return carry

        lax.fori_loop(0, limit, second_kept, 0)
        lax.fori_loop(limit, groups, second_rest, 0)

    for h in range(HALVES):
        part(h)


def middle_kernel(
    capacity, list_ref, size_ref, recv_ref, rows_ref, tiles_ref, mass_ref, part_ref, *scratch
):
    def weights(start, value, weight_ref):
        weight_ref[start : start + value.shape[0], :] = value

    def store(slot, tile, power, weight_ref):
        power = power * weight_ref[pl.ds(tile, 1), :]
        part_ref[pl.ds(slot, 1), :] = jnp.sum(fold_lanes(power).T, axis=0, keepdims=True)

    iterate(
        capacity,
        weights,
        store,
        list_ref,
        size_ref,
        recv_ref,
        rows_ref,
        tiles_ref,
        mass_ref,
        *scratch,
    )


def last_kernel(
    capacity,
    list_ref,
    size_ref,
    recv_ref,
    rows_ref,
    tiles_ref,
    mass_ref,
    sample_ref,
    part_ref,
    *scratch,
):
    *scratch, value_ref = scratch
    row = lax.broadcasted_iota(jnp.int32, (8, TILE), 0)

    def weights(start, value, weight_ref):
        value_ref[start : start + value.shape[0], :] = value

        def body(t, carry):
            where = pl.ds(pl.multiple_of(t * TILE, TILE), TILE)
            place = jnp.ones((8, TILE), f32)
            for d in range(3):
                part = jnp.broadcast_to(sample_ref[d : d + 1, where], (8, TILE)) - 0.5
                place = jnp.where((row == d) | (row == d + 4), part, place)
            high, middle, low = split3(place * value_ref[pl.ds(t, 1), :])
            upper = jnp.where(row < 4, high, middle)
            lower = jnp.where(row < 4, low, 0.0)
            weight_ref[t] = jnp.concatenate([upper, lower], 0).astype(bf16)
            return carry

        lax.fori_loop(start, start + value.shape[0], body, 0, unroll=4)

    def store(slot, tile, power, weight_ref):
        left = weight_ref[tile]
        high = power.astype(bf16)
        low = (power - high.astype(f32)).astype(bf16)
        dims = (((1,), (1,)), ((), ()))
        out = lax.dot_general(left, high, dims, preferred_element_type=f32)
        out = out + lax.dot_general(left, low, dims, preferred_element_type=f32)
        out = out[0:8] + out[8:16]
        part_ref[pl.ds(pl.multiple_of(slot * ROWS, ROWS), ROWS), :] = out[0:4] + out[4:8]

    iterate(
        capacity,
        weights,
        store,
        list_ref,
        size_ref,
        recv_ref,
        rows_ref,
        tiles_ref,
        mass_ref,
        *scratch,
    )


def local(
    positions,
    velocities,
    masses,
    samples,
    sample_mass,
    start_potential,
    route_owner,
    route_tile,
    live_count,
):
    devices = lax.axis_size("dev")
    blocks = route_owner.shape[0]
    tiles = start_potential.shape[0] // TILE
    capacity = 2 * blocks * K // devices
    slots = devices * capacity
    struct = jax.ShapeDtypeStruct

    def exchange(values):
        rows = values.shape[0] // devices
        got = lax.all_to_all(
            values.reshape(devices, rows, BLK), "dev", split_axis=0, concat_axis=0, tiled=True
        )
        return got.reshape(values.shape)

    send, slot = call(
        functools.partial(setup_kernel, capacity),
        (struct((slots * ROWS, BLK), f32), struct((blocks * K,), jnp.int32)),
        [SMEM, SMEM, SMEM, VMEM],
        (VMEM, SMEM),
        [pltpu.SMEM((devices,), jnp.int32)],
        10**6,
        (route_owner.T, route_tile.T, live_count, positions),
        67_000_000,
    )
    recv = exchange(send)
    split_tiles = call(
        sample_kernel,
        struct((tiles, DEPTH, TILE), bf16),
        [VMEM],
        VMEM,
        [],
        10**7,
        (samples,),
        8 * 2**20,
    )
    mass_rows = masses.reshape(blocks, BLK)
    sample_rows = sample_mass.reshape(tiles * CHUNKS, BLK)
    pot_rows = start_potential.reshape(tiles * CHUNKS, BLK)
    part, order, size = call(
        functools.partial(row_first_kernel, capacity),
        (struct((slots, BLK), f32), struct((HALVES * (slots + 2 * G),), jnp.int32), struct((HALVES,), jnp.int32)),
        [VMEM, VMEM, VMEM],
        (VMEM, SMEM, SMEM),
        [
            pltpu.VMEM((tiles, TILE), f32),
            pltpu.VMEM((tiles, BLK), f32),
            pltpu.VMEM((G, BLK, DEPTH), bf16),
            pltpu.VMEM((devices, BLK), jnp.int32),
            pltpu.SMEM((devices, BLK), jnp.int32),
            pltpu.SMEM((slots + 2 * G,), jnp.int32),
            pltpu.SemaphoreType.DMA,
        ],
        10**9,
        (recv, split_tiles, pot_rows),
        16 * 2**20,
    )
    part = exchange(part)
    row_scratch = [pltpu.VMEM((K, blocks, BLK), f32)]
    send, row = call(
        home_first_kernel,
        (struct((slots, BLK), f32), struct((blocks, BLK), f32)),
        [SMEM, SMEM, VMEM, VMEM],
        (VMEM, VMEM),
        row_scratch,
        10**6,
        (slot, live_count, part, mass_rows),
        4 * 2**20,
    )
    rows = exchange(send)
    scratch = [
        pltpu.VMEM((min(KEPT, slots), BLK, TILE), f32),
        pltpu.VMEM((G, BLK, DEPTH), bf16),
        pltpu.VMEM((tiles + 1, 8, TILE), f32),
        pltpu.VMEM((tiles, BLK), f32),
    ]
    values = pltpu.VMEM((tiles, TILE), f32)
    part = call(
        functools.partial(middle_kernel, capacity),
        struct((slots, BLK), f32),
        [SMEM, SMEM] + [VMEM] * 4,
        VMEM,
        scratch + [values],
        10**9,
        (order, size, recv, rows, split_tiles, sample_rows),
    )
    part = exchange(part)
    send = call(
        home_next_kernel,
        struct((slots, BLK), f32),
        [SMEM, SMEM, VMEM, VMEM, VMEM],
        VMEM,
        [pltpu.VMEM((blocks, BLK), f32)] + row_scratch,
        10**6,
        (slot, live_count, part, mass_rows, row),
        4 * 2**20,
    )
    rows = exchange(send)
    part = call(
        functools.partial(last_kernel, capacity),
        struct((slots * ROWS, BLK), f32),
        [SMEM, SMEM] + [VMEM] * 5,
        VMEM,
        scratch + [pltpu.VMEM((tiles, 16, TILE), bf16), values],
        10**9,
        (order, size, recv, rows, split_tiles, sample_rows, samples),
    )
    part = exchange(part)
    return call(
        home_last_kernel,
        (struct(positions.shape, f32), struct(positions.shape, f32)),
        [SMEM, SMEM, VMEM, VMEM, VMEM],
        (VMEM, VMEM),
        [],
        10**6,
        (slot, live_count, part, positions, velocities),
        4 * 2**20,
    )


def solution(mesh):
    placed = (
        P(None, "dev"),
        P(None, "dev"),
        P("dev"),
        P(None, "dev"),
        P("dev"),
        P("dev"),
        P("dev", None),
        P("dev", None),
        P("dev"),
    )
    return jax.shard_map(
        local,
        mesh=mesh,
        in_specs=placed,
        out_specs=(P(None, "dev"), P(None, "dev")),
        check_vma=False,
    )
```

```python
import functools
import jax
import jax.numpy as jnp
from jax import lax
from jax.experimental import pallas as pl
from jax.experimental.pallas import tpu as pltpu
from jax.sharding import PartitionSpec as P

BLK = 128
TILE = 512
K = 4
CHUNKS = TILE // BLK
EPSILON = 0.01
STIFFNESS = 150.0
TIMESTEP = 0.05
LOG2E = 1.4426950408889634
SCALE = LOG2E / EPSILON
NEGATIVE = -1e30
ROW_SHIFT = 115.0
COL_SHIFT = 110.0
G = 16
KEPT = 144
HALVES = 2
ROWS = 4
DEPTH = 32
PACK = BLK // DEPTH

LARGE = 44 * 2**20
f32 = jnp.float32
bf16 = jnp.bfloat16
VMEM = pl.BlockSpec(memory_space=pltpu.VMEM)
SMEM = pl.BlockSpec(memory_space=pltpu.SMEM)


def call(kernel, out_shape, in_specs, out_specs, scratch, flops, args, limit=LARGE):
    size = sum(a.size * a.dtype.itemsize for a in args)
    return pl.pallas_call(
        kernel,
        out_shape=out_shape,
        in_specs=in_specs,
        out_specs=out_specs,
        scratch_shapes=scratch,
        compiler_params=pltpu.CompilerParams(vmem_limit_bytes=limit),
        cost_estimate=pl.CostEstimate(flops=flops, bytes_accessed=size, transcendentals=0),
    )(*args)


def split3(value):
    high = value.astype(bf16).astype(f32)
    rest = value - high
    middle = rest.astype(bf16).astype(f32)
    return high, middle, rest - middle


def setup_kernel(capacity, owner_ref, tile_ref, live_ref, pos_ref, send_ref, slot_ref, count_ref):
    blocks = live_ref.shape[0]
    stride = capacity * ROWS

    def clear(i, carry):
        count_ref[i] = 0
        return carry

    lax.fori_loop(0, count_ref.shape[0], clear, 0)
    send_ref[...] = jnp.full(send_ref.shape, -1.0, f32)
    for b in range(blocks):
        rows = [pos_ref[d : d + 1, b * BLK : (b + 1) * BLK] for d in range(3)]
        for k in range(K):
            owner = owner_ref[k, b]
            rank = count_ref[owner]
            count_ref[owner] = rank + 1
            slot_ref[b * K + k] = owner * capacity + rank
            tile = jnp.where(k < live_ref[b], tile_ref[k, b], -1).astype(f32)
            base = owner * stride + rank
            for d in range(3):
                send_ref[pl.ds(base + d * capacity, 1), :] = rows[d]
            send_ref[pl.ds(base + 3 * capacity, 1), :] = jnp.full((1, BLK), tile, f32)


def home_gather(slot_ref, live_ref, recv_ref, parts_ref, filler):
    blocks = live_ref.shape[0]
    for b in range(blocks):
        live = live_ref[b]
        for k in range(K):
            row = recv_ref[pl.ds(slot_ref[b * K + k], 1), :]
            parts_ref[k, b : b + 1, :] = jnp.where(k < live, row, filler)


def home_scatter(slot_ref, rows_ref, send_ref):
    for b in range(rows_ref.shape[0]):
        row = rows_ref[b : b + 1, :]
        for k in range(K):
            send_ref[pl.ds(slot_ref[b * K + k], 1), :] = row


def home_first_kernel(slot_ref, live_ref, recv_ref, mass_ref, send_ref, row_ref, parts_ref):
    home_gather(slot_ref, live_ref, recv_ref, parts_ref, NEGATIVE)
    parts = parts_ref[...]
    top = jnp.max(parts, axis=0)
    total = jnp.sum(jnp.exp2(parts - top[None]), axis=0)
    row_ref[...] = jnp.log2(mass_ref[...]) - (top + jnp.log2(total))
    home_scatter(slot_ref, row_ref, send_ref)


def home_next_kernel(slot_ref, live_ref, recv_ref, mass_ref, old_ref, send_ref, row_ref, parts_ref):
    home_gather(slot_ref, live_ref, recv_ref, parts_ref, 0.0)
    total = jnp.sum(parts_ref[...], axis=0)
    row_ref[...] = old_ref[...] + jnp.log2(mass_ref[...]) - jnp.log2(total)
    home_scatter(slot_ref, row_ref, send_ref)


def home_last_kernel(slot_ref, live_ref, recv_ref, pos_ref, vel_ref, new_pos_ref, new_vel_ref):
    blocks = live_ref.shape[0]
    for b in range(blocks):
        live = live_ref[b]
        parts = jnp.zeros((ROWS, BLK), f32)
        for k in range(K):
            rows = recv_ref[pl.ds(slot_ref[b * K + k] * ROWS, ROWS), :]
            parts = parts + jnp.where(k < live, rows, 0.0)
        where = slice(b * BLK, (b + 1) * BLK)
        centre = parts[0:3] / parts[3:4] + 0.5
        here = pos_ref[:, where]
        velocity = vel_ref[:, where] + STIFFNESS * (centre - here)
        new_vel_ref[:, where] = velocity
        new_pos_ref[:, where] = here + TIMESTEP * velocity


def sample_rows(sample_ref, t, extra, row):
    where = pl.ds(pl.multiple_of(t * TILE, TILE), TILE)
    parts = [jnp.broadcast_to(sample_ref[d : d + 1, where], (8, TILE)) - 0.5 for d in range(3)]
    square = parts[0] * parts[0] + parts[1] * parts[1] + parts[2] * parts[2]
    value = (-0.5 * SCALE) * square
    if extra is not None:
        value = value + extra
    for d in range(3):
        value = jnp.where((row == d) | (row == d + 5), parts[d], value)
    high, middle, low = split3(value)
    one = row == 3
    first = jnp.where(one, 1.0, jnp.where(row > 4, middle, high))
    second = jnp.where(one, 1.0, jnp.where(row > 4, low, middle))
    third = jnp.where(one, 1.0, jnp.where(row == 4, low, high))
    return jnp.concatenate([first, second, third, jnp.zeros_like(first)], 0)


def sample_kernel(sample_ref, pot_ref, tiles_ref, turned_ref, top_ref, beta_ref):
    row = lax.broadcasted_iota(jnp.int32, (8, TILE), 0)
    pot = lanes_of(pot_ref) * SCALE
    top = jnp.max(pot, axis=1, keepdims=True)
    beta_ref[...] = pot - top
    top_ref[...] = jnp.broadcast_to(top - ROW_SHIFT, top_ref.shape)

    def body(q, carry):
        sides = []
        for i in range(PACK):
            t = q * PACK + i
            tiles_ref[t] = sample_rows(sample_ref, t, None, row).astype(bf16)
            sides.append(sample_rows(sample_ref, t, beta_ref[pl.ds(t, 1), :], row))
        turned_ref[q] = jnp.concatenate(sides, 0).astype(bf16).T
        return carry

    lax.fori_loop(0, turned_ref.shape[0], body, 0)


def lanes_of(ref):
    tiles = ref.shape[0] // CHUNKS
    return jnp.concatenate([ref[pl.ds(c, tiles, stride=CHUNKS), :] for c in range(CHUNKS)], 1)


def particle_rows(recv_ref, place, extra, row):
    base, capacity = place
    parts = [
        (jnp.broadcast_to(recv_ref[pl.ds(base + d * capacity, 1), :], (8, BLK)) - 0.5)
        for d in range(3)
    ]
    square = parts[0] * parts[0] + parts[1] * parts[1] + parts[2] * parts[2]
    value = (-0.5 * SCALE) * square + extra
    for d in range(3):
        value = jnp.where((row == d) | (row == d + 5), SCALE * parts[d], value)
    high, middle, low = split3(value)
    one = row == 4
    first = jnp.where(one, 1.0, jnp.where(row > 4, middle, high))
    second = jnp.where(one, 1.0, jnp.where(row == 3, middle, high))
    third = jnp.where(one, 1.0, jnp.where(row < 3, middle, low))
    zero = jnp.zeros_like(first)
    return jnp.concatenate([first, second, third, zero], 0).astype(bf16)


def fold_lanes(value):
    out = value[:, :BLK]
    for c in range(1, CHUNKS):
        out = out + value[:, c * BLK : (c + 1) * BLK]
    return out


def product(left, right):
    return jnp.dot(left, right, preferred_element_type=f32)


def unpack(list_ref, index, capacity):
    code = list_ref[index]
    slot = lax.shift_right_logical(code, 16)
    device = lax.div(slot, capacity)
    return slot, code & 0xFFFF, slot + device * (capacity * (ROWS - 1))


def part_start(h, slots):
    return h * (slots + 2 * G)


def listed(list_ref, start, capacity):
    slots = [unpack(list_ref, start + k, capacity) for k in range(G)]
    return [list(item) for item in zip(*slots)]


def row_first_kernel(
    capacity,
    recv_ref,
    turned_ref,
    top_ref,
    part_ref,
    list_ref,
    size_ref,
    right_ref,
    asked_ref,
    tile_ref,
    all_ref,
    sem,
):
    devices = asked_ref.shape[0]
    lane = lax.broadcasted_iota(jnp.int32, (devices, capacity, BLK), 2)
    rank = lax.broadcasted_iota(jnp.int32, (devices, capacity, BLK), 1)
    asked = recv_ref[...].reshape(devices, ROWS * capacity, BLK)[:, 3 * capacity :, :]
    asked_ref[...] = jnp.sum(jnp.where(lane == rank, asked, 0.0), axis=1).astype(jnp.int32)
    copy = pltpu.make_async_copy(asked_ref, tile_ref, sem)
    copy.start()

    row = lax.broadcasted_iota(jnp.int32, (8, BLK), 0)
    copy.wait()

    slots = devices * capacity
    half = top_ref.shape[0] // HALVES

    def compact(device, counts):
        for k in range(capacity):
            tile = tile_ref[device, k]
            upper = tile >= half
            code = ((device * capacity + k) << 16) + jnp.maximum(tile, 0)
            all_ref[counts[0] + counts[1]] = code
            place = jnp.where(upper, part_start(1, slots) + counts[1], counts[0])
            list_ref[place] = code
            low = jnp.where((tile >= 0) & (tile < half), 1, 0)
            counts = (counts[0] + low, counts[1] + jnp.where(upper, 1, 0))
        return counts

    zero = jnp.int32(0)
    counts = lax.fori_loop(0, devices, compact, (zero, zero))
    for h in range(HALVES):
        size_ref[h] = counts[h]
        start = part_start(h, slots)
        list_ref[start + counts[h]] = 0
        for k in range(G):
            list_ref[start + counts[h] + k] = list_ref[start]

    count = counts[0] + counts[1]
    groups = (count + G - 1) // G
    all_ref[count] = 0
    for k in range(G):
        all_ref[count + k] = all_ref[0]

    def prepare(g):
        slot, tile, base = listed(all_ref, g * G, capacity)
        for k in range(G):
            side = particle_rows(recv_ref, (base[k], capacity), ROW_SHIFT, row)
            at = tile[k] % PACK
            sides = [jnp.where(at == i, side, jnp.zeros_like(side)) for i in range(PACK)]
            right_ref[k] = jnp.concatenate(sides, 0)

    prepare(0)

    def body(g, carry):
        slot, tile, base = listed(all_ref, g * G, capacity)
        power = [jnp.exp2(product(turned_ref[tile[k] // PACK], right_ref[k])) for k in range(G)]
        prepare(jnp.minimum(g + 1, groups - 1))
        for k in range(G):
            total = jnp.sum(jnp.sum(power[k].reshape(TILE // 8, 8, BLK), axis=0), axis=0)
            part_ref[pl.ds(slot[k], 1), :] = jnp.log2(total[None]) + top_ref[pl.ds(tile[k], 1), :]
        return carry

    lax.fori_loop(0, groups, body, 0)


def iterate(
    capacity,
    weights,
    store,
    list_ref,
    size_ref,
    recv_ref,
    rows_ref,
    tiles_ref,
    mass_ref,
    kept_ref,
    left_ref,
    sums_ref,
    peak_ref,
    weight_ref,
):
    tiles = tiles_ref.shape[0]
    slots = rows_ref.shape[0]
    half = tiles // HALVES
    row = lax.broadcasted_iota(jnp.int32, (8, BLK), 0)
    peak_ref[...] = jnp.full(peak_ref.shape, NEGATIVE, f32)
    sums_ref[...] = jnp.zeros(sums_ref.shape, f32)
    mass = lanes_of(mass_ref)

    for h in range(HALVES):

        def find(g, carry, start=part_start(h, slots)):
            slot, tile, base = listed(list_ref, start + g * G, capacity)
            for k in range(G):
                at = pl.ds(tile[k], 1)
                peak_ref[at, :] = jnp.maximum(peak_ref[at, :], rows_ref[pl.ds(slot[k], 1), :])
            return carry

        lax.fori_loop(0, (size_ref[h] + G - 1) // G, find, 0)
    peak = jnp.max(peak_ref[...], axis=1, keepdims=True)
    peak_ref[...] = jnp.broadcast_to(COL_SHIFT - peak, peak_ref.shape)

    def part(h):
        start = part_start(h, slots)
        count = size_ref[h]
        groups = (count + G - 1) // G
        limit = jnp.minimum(groups, kept_ref.shape[0] // G)

        def prepare(g):
            slot, tile, base = listed(list_ref, start + g * G, capacity)
            for k in range(G):
                extra = rows_ref[pl.ds(slot[k], 1), :] + peak_ref[pl.ds(tile[k], 1), :]
                extra = jnp.broadcast_to(extra, (8, BLK))
                left_ref[k] = particle_rows(recv_ref, (base[k], capacity), extra, row).T

        def power(k, tile):
            return jnp.exp2(product(left_ref[k], tiles_ref[tile[k]]))

        def first(keep, g, carry):
            slot, tile, base = listed(list_ref, start + g * G, capacity)
            raised = [power(k, tile) for k in range(G)]
            prepare(jnp.minimum(g + 1, groups - 1))
            for k in range(G):
                if keep:
                    kept_ref[g * G + k] = raised[k]
                into = jnp.where(g * G + k < count, tile[k], tiles)
                sums_ref[into] += jnp.sum(raised[k].reshape(BLK // 8, 8, TILE), axis=0)
            return carry

        prepare(0)
        lax.fori_loop(0, limit, functools.partial(first, True), 0)
        lax.fori_loop(limit, groups, functools.partial(first, False), 0)
        here = slice(h * half, (h + 1) * half)
        total = jnp.sum(sums_ref[here], axis=1)
        weights(h * half, mass[here] / total, weight_ref)

        def second_kept(g, carry):
            slot, tile, base = listed(list_ref, start + g * G, capacity)
            for k in range(G):
                store(slot[k], tile[k], kept_ref[g * G + k], weight_ref)
            return carry

        def second_rest(g, carry):
            slot, tile, base = listed(list_ref, start + g * G, capacity)
            prepare(g)
            for k in range(G):
                store(slot[k], tile[k], power(k, tile), weight_ref)
            return carry

        lax.fori_loop(0, limit, second_kept, 0)
        lax.fori_loop(limit, groups, second_rest, 0)

    for h in range(HALVES):
        part(h)


def middle_kernel(
    capacity, list_ref, size_ref, recv_ref, rows_ref, tiles_ref, mass_ref, part_ref, *scratch
):
    def weights(start, value, weight_ref):
        weight_ref[start : start + value.shape[0], :] = value

    def store(slot, tile, power, weight_ref):
        power = power * weight_ref[pl.ds(tile, 1), :]
        part_ref[pl.ds(slot, 1), :] = jnp.sum(fold_lanes(power).T, axis=0, keepdims=True)

    iterate(
        capacity,
        weights,
        store,
        list_ref,
        size_ref,
        recv_ref,
        rows_ref,
        tiles_ref,
        mass_ref,
        *scratch,
    )


def last_kernel(
    capacity,
    list_ref,
    size_ref,
    recv_ref,
    rows_ref,
    tiles_ref,
    mass_ref,
    sample_ref,
    part_ref,
    *scratch,
):
    *scratch, value_ref = scratch
    row = lax.broadcasted_iota(jnp.int32, (8, TILE), 0)

    def weights(start, value, weight_ref):
        value_ref[start : start + value.shape[0], :] = value

        def body(t, carry):
            where = pl.ds(pl.multiple_of(t * TILE, TILE), TILE)
            place = jnp.ones((8, TILE), f32)
            for d in range(3):
                part = jnp.broadcast_to(sample_ref[d : d + 1, where], (8, TILE)) - 0.5
                place = jnp.where((row == d) | (row == d + 4), part, place)
            high, middle, low = split3(place * value_ref[pl.ds(t, 1), :])
            upper = jnp.where(row < 4, high, middle)
            lower = jnp.where(row < 4, low, 0.0)
            weight_ref[t] = jnp.concatenate([upper, lower], 0).astype(bf16)
            return carry

        lax.fori_loop(start, start + value.shape[0], body, 0, unroll=4)

    def store(slot, tile, power, weight_ref):
        left = weight_ref[tile]
        high = power.astype(bf16)
        low = (power - high.astype(f32)).astype(bf16)
        dims = (((1,), (1,)), ((), ()))
        out = lax.dot_general(left, high, dims, preferred_element_type=f32)
        out = out + lax.dot_general(left, low, dims, preferred_element_type=f32)
        out = out[0:8] + out[8:16]
        part_ref[pl.ds(pl.multiple_of(slot * ROWS, ROWS), ROWS), :] = out[0:4] + out[4:8]

    iterate(
        capacity,
        weights,
        store,
        list_ref,
        size_ref,
        recv_ref,
        rows_ref,
        tiles_ref,
        mass_ref,
        *scratch,
    )


def local(
    positions,
    velocities,
    masses,
    samples,
    sample_mass,
    start_potential,
    route_owner,
    route_tile,
    live_count,
):
    devices = lax.axis_size("dev")
    blocks = route_owner.shape[0]
    tiles = start_potential.shape[0] // TILE
    capacity = 2 * blocks * K // devices
    slots = devices * capacity
    struct = jax.ShapeDtypeStruct

    def exchange(values):
        rows = values.shape[0] // devices
        got = lax.all_to_all(
            values.reshape(devices, rows, BLK), "dev", split_axis=0, concat_axis=0, tiled=True
        )
        return got.reshape(values.shape)

    send, slot = call(
        functools.partial(setup_kernel, capacity),
        (struct((slots * ROWS, BLK), f32), struct((blocks * K,), jnp.int32)),
        [SMEM, SMEM, SMEM, VMEM],
        (VMEM, SMEM),
        [pltpu.SMEM((devices,), jnp.int32)],
        10**6,
        (route_owner.T, route_tile.T, live_count, positions),
        67_000_000,
    )
    recv = exchange(send)
    pot_rows = start_potential.reshape(tiles * CHUNKS, BLK)
    split_tiles, turned, top = call(
        sample_kernel,
        (
            struct((tiles, DEPTH, TILE), bf16),
            struct((tiles // PACK, TILE, BLK), bf16),
            struct((tiles, BLK), f32),
        ),
        [VMEM, VMEM],
        (VMEM, VMEM, VMEM),
        [pltpu.VMEM((tiles, TILE), f32)],
        10**7,
        (samples, pot_rows),
        10 * 2**20,
    )
    mass_rows = masses.reshape(blocks, BLK)
    weight_rows = sample_mass.reshape(tiles * CHUNKS, BLK)
    part, order, size = call(
        functools.partial(row_first_kernel, capacity),
        (struct((slots, BLK), f32), struct((HALVES * (slots + 2 * G),), jnp.int32), struct((HALVES,), jnp.int32)),
        [VMEM, VMEM, VMEM],
        (VMEM, SMEM, SMEM),
        [
            pltpu.VMEM((G, BLK, BLK), bf16),
            pltpu.VMEM((devices, BLK), jnp.int32),
            pltpu.SMEM((devices, BLK), jnp.int32),
            pltpu.SMEM((slots + 2 * G,), jnp.int32),
            pltpu.SemaphoreType.DMA,
        ],
        10**9,
        (recv, turned, top),
        8 * 2**20,
    )
    part = exchange(part)
    row_scratch = [pltpu.VMEM((K, blocks, BLK), f32)]
    send, row = call(
        home_first_kernel,
        (struct((slots, BLK), f32), struct((blocks, BLK), f32)),
        [SMEM, SMEM, VMEM, VMEM],
        (VMEM, VMEM),
        row_scratch,
        10**6,
        (slot, live_count, part, mass_rows),
        4 * 2**20,
    )
    rows = exchange(send)
    scratch = [
        pltpu.VMEM((min(KEPT, slots), BLK, TILE), f32),
        pltpu.VMEM((G, BLK, DEPTH), bf16),
        pltpu.VMEM((tiles + 1, 8, TILE), f32),
        pltpu.VMEM((tiles, BLK), f32),
    ]
    values = pltpu.VMEM((tiles, TILE), f32)
    part = call(
        functools.partial(middle_kernel, capacity),
        struct((slots, BLK), f32),
        [SMEM, SMEM] + [VMEM] * 4,
        VMEM,
        scratch + [values],
        10**9,
        (order, size, recv, rows, split_tiles, weight_rows),
    )
    part = exchange(part)
    send = call(
        home_next_kernel,
        struct((slots, BLK), f32),
        [SMEM, SMEM, VMEM, VMEM, VMEM],
        VMEM,
        [pltpu.VMEM((blocks, BLK), f32)] + row_scratch,
        10**6,
        (slot, live_count, part, mass_rows, row),
        4 * 2**20,
    )
    rows = exchange(send)
    part = call(
        functools.partial(last_kernel, capacity),
        struct((slots * ROWS, BLK), f32),
        [SMEM, SMEM] + [VMEM] * 5,
        VMEM,
        scratch + [pltpu.VMEM((tiles, 16, TILE), bf16), values],
        10**9,
        (order, size, recv, rows, split_tiles, weight_rows, samples),
    )
    part = exchange(part)
    return call(
        home_last_kernel,
        (struct(positions.shape, f32), struct(positions.shape, f32)),
        [SMEM, SMEM, VMEM, VMEM, VMEM],
        (VMEM, VMEM),
        [],
        10**6,
        (slot, live_count, part, positions, velocities),
        4 * 2**20,
    )


def solution(mesh):
    placed = (
        P(None, "dev"),
        P(None, "dev"),
        P("dev"),
        P(None, "dev"),
        P("dev"),
        P("dev"),
        P("dev", None),
        P("dev", None),
        P("dev"),
    )
    return jax.shard_map(
        local,
        mesh=mesh,
        in_specs=placed,
        out_specs=(P(None, "dev"), P(None, "dev")),
        check_vma=False,
    )
```
